128 devices in a mesh: segment: 2 (over y_lo), space: 32 (over x, z, core), mirror: 2 (over y_hi).
Axes of the slice: x: 4, y: 4 (y_hi: 2, y_lo: 2; y = y_hi * 2 + y_lo), z: 4, core: 2. Of those that a mesh axis runs over, the one named last changes fastest.
Arguments:
- arrivals: bfloat16 [2, 2, 512, 128, 256], P('mirror', 'segment', 'space'), may hold values from -6 to 6
- stashed: bfloat16 [2, 2, 512, 128, 256], P('mirror', 'segment', 'space'), may hold values from -6 to 6
- weights: bfloat16 [2, 2, 2, 3, 3, 256, 256], P('mirror', 'segment'), may hold values from -0.125 to 0.125
Outputs:
- departures: bfloat16 [2, 2, 512, 128, 256], P('mirror', 'segment', 'space')
- grad_sum: float32 [2, 2, 256, 2, 3, 3, 256], P('mirror', 'segment', 'space')
The draws below stay inside these ranges and needn't reach their ends.
All inputs are finite; a program needn't handle non-finite values.
Results may differ from the reference program's by a relative error of at most 0.0053.
Values may be sent and summed in bfloat16 or wider, within the bound.
No kernel may reach another device: no remote copies, remote signals or barrier semaphores. Data moves between devices by JAX's collectives and lax.ppermute only.
A program may use at most 128 MiB of HBM per device.

```python
import jax
import jax.numpy as jnp
from jax import lax

C = 256
CONVS = 2
COLS = 128
ROWS = 512
N_SEGMENT = 2
N_MIRROR = 2


def raised(values, rng, source, target, blocks, factor):
    owner, partner = [(jnp.arange(values.shape[position]) // (values.shape[position] // blocks)).reshape([-1 if axis == position else 1 for axis in range(values.ndim)]) for position in (source, target)]
    chosen = jax.random.permutation(rng, blocks)[partner]
    strong = (owner == chosen) | (owner == (partner + blocks // 2) % blocks)
    return jnp.where(strong, factor * values, values)


def shard_levels(key, shape, split, least, top_value):
    factor_of, own = 1.0, jax.random.fold_in(key, 6)
    for dim, parts in split:
        steps = jnp.exp(jax.random.uniform(jax.random.fold_in(own, dim), (parts,), jnp.float32, least / len(split), top_value / len(split)))
        factor_of = factor_of * jnp.repeat(steps, shape[dim] // parts).reshape([-1 if axis == dim else 1 for axis in range(len(shape))])
    return factor_of


def noise(key, extent, scale, limit, split=(), held_as=jnp.bfloat16):
    level = shard_levels(key, extent, split, -0.22, 0.18) if split else 1.0
    result = jax.random.normal(key, extent, jnp.float32) * scale * level
    return jnp.minimum(jnp.maximum(result, -limit), limit).astype(held_as)


def bell_draw_with(own_key, dims, spread, reach, pieces, heavy, kind=jnp.bfloat16):
    result = spread * jax.random.normal(own_key, dims, jnp.float32)
    if pieces:
        result = result * shard_levels(own_key, dims, pieces, -0.22, 0.18)
    return jnp.clip(raised(result, jax.random.fold_in(own_key, 3), *heavy), -reach, reach).astype(kind)


def setup_inputs(seed: int = 0) -> dict:
    seeds = jax.random.split(jax.random.key(seed), 4)
    return {
        "arrivals": noise(seeds[0], (N_MIRROR, N_SEGMENT, ROWS, COLS, C), 1.0, 6.0, ((0, 2), (1, 2), (2, 32))),
        "stashed": bell_draw_with(seeds[1], (N_MIRROR, N_SEGMENT, ROWS, COLS, C), 1.0, 6.0, ((0, 2), (1, 2), (2, 32)), (2, 4, 32, 2.75)),
        "weights": noise(seeds[2], (N_MIRROR, N_SEGMENT, CONVS, 3, 3, C, C), (9 * C) ** -0.5, 0.125, ((0, 2), (1, 2))),
    }


def convolve(padded, kernel):
    row_count = padded.shape[0] - 2
    col_count = padded.shape[1]
    widened = jnp.pad(padded, ((0, 0), (1, 1), (0, 0)))
    channels = kernel.shape[3]
    summed = jnp.zeros((row_count * col_count, channels), jnp.float32)
    for row_shift in range(3):
        for col_shift in range(3):
            window = widened[row_shift:row_shift + row_count, col_shift:col_shift + col_count].reshape(row_count * col_count, -1)
            summed = summed + jnp.dot(window, kernel[row_shift, col_shift], preferred_element_type=jnp.float32)
    return summed.reshape(row_count, col_count, channels)

def weight_grad(padded, cotangent):
    row_count = cotangent.shape[0]
    col_count = cotangent.shape[1]
    widened = jnp.pad(padded, ((0, 0), (1, 1), (0, 0)))
    flat_grad = cotangent.reshape(row_count * col_count, -1)
    entries = []
    for row_shift in range(3):
        row_list = []
        for col_shift in range(3):
            window = widened[row_shift:row_shift + row_count, col_shift:col_shift + col_count].reshape(row_count * col_count, -1)
            row_list.append(lax.dot_general(window, flat_grad, (((0,), (0,)), ((), ())), preferred_element_type=jnp.float32))
        entries.append(jnp.stack(row_list, axis=1))
    return jnp.stack(entries, axis=1)

def flipped(kernel):
    return jnp.transpose(kernel[::-1, ::-1], (0, 1, 3, 2))

def silu_slope(pre_act):
    sigmoid_val = jax.nn.sigmoid(pre_act)
    return sigmoid_val * (1.0 + pre_act * (1.0 - sigmoid_val))

def rows_padded(field_in):
    return jnp.pad(field_in, ((1, 1), (0, 0), (0, 0)))

def forward_section(field_in, kernels):
    pre_act = convolve(rows_padded(field_in), kernels[0])
    hidden = jax.nn.silu(pre_act).astype(jnp.bfloat16)
    return (field_in.astype(jnp.float32) + convolve(rows_padded(hidden), kernels[1])).astype(jnp.bfloat16)

def backward_section(field_in, cotangent, kernels, grad_scale):
    pre_act = convolve(rows_padded(field_in), kernels[0])
    hidden = jax.nn.silu(pre_act).astype(jnp.bfloat16)
    second = weight_grad(rows_padded(hidden), cotangent)
    inner_grad = (convolve(rows_padded(cotangent), flipped(kernels[1])) * silu_slope(pre_act)).astype(jnp.bfloat16)
    first = weight_grad(rows_padded(field_in), inner_grad)
    entering = (cotangent.astype(jnp.float32) + convolve(rows_padded(inner_grad), flipped(kernels[0]))).astype(jnp.bfloat16)
    return (entering, jnp.stack((first, second), axis=1) * grad_scale)

def reference(arrivals, stashed, weights):
    row_total = arrivals.shape[2]
    col_total = arrivals.shape[3]
    grad_scale = 1.0 / (row_total * col_total) ** 0.5
    leaving = [[None, None], [None, None]]
    grads = [[None, None], [None, None]]
    for replica in range(2):
        lead_pos = 0 if replica == 0 else 1
        tail_pos = 1 - lead_pos
        middle = forward_section(arrivals[replica, lead_pos], weights[replica, lead_pos])
        leaving[replica][tail_pos] = forward_section(middle, weights[replica, tail_pos])
        back_grad, grads[replica][tail_pos] = backward_section(stashed[replica, tail_pos], arrivals[replica, tail_pos], weights[replica, tail_pos], grad_scale)
        leaving[replica][lead_pos], grads[replica][lead_pos] = backward_section(stashed[replica, lead_pos], back_grad, weights[replica, lead_pos], grad_scale)
    departures = jnp.stack([jnp.stack(leaving[replica]) for replica in range(2)])
    totals = jnp.stack([jnp.stack([grads[replica][place] + grads[1 - replica][1 - place] for place in range(2)]) for replica in range(2)])
    return (departures, totals)
```

```python
import functools
import math

import jax
import jax.numpy as jnp
from jax import lax
from jax.experimental import pallas as pl
from jax.experimental.pallas import tpu as pltpu
from jax.sharding import Mesh
from jax.sharding import PartitionSpec as P

SPACE = ("space_0", "space_1", "space_2")
BF16 = jnp.bfloat16
F32 = jnp.float32
COLS = 128
CH = 256
TAPS = 9 * CH
MIB = 1 << 20


def rows(first, count):
    return pl.ds(first * COLS, count * COLS)


def store3(dst, row, val, count):
    size = count * COLS
    col = lax.broadcasted_iota(jnp.int32, (size, CH), 0) & (COLS - 1)
    val = val.astype(F32)
    left = jnp.where(col == 0, 0.0, pltpu.roll(val, 1, 0))
    right = jnp.where(col == COLS - 1, 0.0, pltpu.roll(val, size - 1, 0))
    where = rows(row, count)
    dst[where, 0:CH] = left.astype(BF16)
    dst[where, CH : 2 * CH] = val.astype(BF16)
    dst[where, 2 * CH :] = right.astype(BF16)


def fill3(dst, row, src, first, count):
    for step in range(0, count, 2):
        size = min(2, count - step)
        store3(dst, row + step, src[rows(first + step, size), :], size)


def conv(src3, first, count, weights, which, transposed):
    total = None
    for a in range(3):
        for b in range(3):
            window = src3[rows(first + a, count), b * CH : (b + 1) * CH]
            if transposed:
                part = lax.dot_general(
                    window,
                    weights[which, 2 - a, 2 - b],
                    (((1,), (1,)), ((), ())),
                    preferred_element_type=F32,
                )
            else:
                part = jnp.dot(window, weights[which, a, b], preferred_element_type=F32)
            total = part if total is None else total + part
    return total


def outer(left, right):
    return lax.dot_general(left, right, (((0,), (0,)), ((), ())), preferred_element_type=F32)


def put_grad(dst, conv_index, a, val):
    for b in range(3):
        at = conv_index * TAPS + (3 * a + b) * CH
        dst[:, at : at + CH] = val[:, (2 - b) * CH : (3 - b) * CH]


def get_grad(src, conv_index, a):
    parts = []
    for b in (2, 1, 0):
        at = conv_index * TAPS + (3 * a + b) * CH
        parts.append(src[:, at : at + CH])
    return jnp.concatenate(parts, axis=1)


def activate(pre):
    sig = jax.nn.sigmoid(pre)
    return pre * sig, sig * (1.0 + pre * (1.0 - sig))


def is_leading():
    return lax.axis_index("segment") == lax.axis_index("mirror")


def by_role(body):
    leading = is_leading()

    @pl.when(leading)
    def _():
        body(True)

    @pl.when(jnp.logical_not(leading))
    def _():
        body(False)


def edge_flags():
    place = lax.axis_index(SPACE)
    count = lax.axis_size(SPACE)
    return (place > 0).astype(F32), (place < count - 1).astype(F32)


def kernel_a(arr, sta, w, out_m, act_m, hid_m, slope_m, s3, a3, c3):
    def body(leading):
        fill3(s3, 0, sta, 2, 12)
        fill3(a3, 0, arr, 2, 12)
        for row in (0, 5):
            pre = conv(s3, row, 5, w, 0, False)
            hid, slope = activate(pre)
            hid_m[rows(row, 5), :] = hid.astype(BF16)
            slope_m[rows(row, 5), :] = slope
            if leading:
                act, _ = activate(conv(a3, row, 5, w, 0, False))
            else:
                act = conv(a3, row, 5, w, 1, True) * slope
            act_m[rows(row, 5), :] = act.astype(BF16)
            store3(c3, row, act, 5)
        for row in (0, 4):
            total = conv(c3, row, 4, w, 1 if leading else 0, not leading)
            out_m[rows(row, 4), :] = (total + arr[rows(4 + row, 4), :].astype(F32)).astype(BF16)

    by_role(body)


def kernel_b(arr, sta, up, down, act_m, w, out_e, act_e, hid_e, slope_e, s3, a3, c3):
    has_up, has_down = edge_flags()

    def body(leading):
        for half in range(2):
            if half == 0:
                store3(s3, 0, up[1], 2)
                fill3(s3, 2, sta, 0, 4)
                store3(a3, 0, up[0], 2)
                fill3(a3, 2, arr, 0, 4)
            else:
                fill3(s3, 6, sta, 12, 4)
                store3(s3, 10, down[1], 2)
                fill3(a3, 6, arr, 12, 4)
                store3(a3, 10, down[0], 2)
            pre = conv(s3, 6 * half, 4, w, 0, False)
            hid, slope = activate(pre)
            spot = lax.broadcasted_iota(jnp.int32, (4 * COLS, CH), 0) // COLS
            if half == 0:
                mask = jnp.where(spot == 0, has_up, 1.0)
            else:
                mask = jnp.where(spot == 3, has_down, 1.0)
            hid_e[rows(4 * half, 4), :] = (hid * mask).astype(BF16)
            slope_e[rows(4 * half, 4), :] = slope
            if leading:
                act, _ = activate(conv(a3, 6 * half, 4, w, 0, False))
            else:
                act = conv(a3, 6 * half, 4, w, 1, True) * slope
            act = act * mask
            act_e[rows(4 * half, 4), :] = act.astype(BF16)
            if half == 0:
                store3(c3, 0, act, 4)
                fill3(c3, 4, act_m, 0, 2)
            else:
                fill3(c3, 6, act_m, 8, 2)
                store3(c3, 8, act, 4)
            total = conv(c3, 6 * half, 4, w, 1 if leading else 0, not leading)
            kept = arr[rows(12 * half, 4), :].astype(F32)
            out_e[rows(4 * half, 4), :] = (total + kept).astype(BF16)

    by_role(body)


def kernel_c(
    got_m, arr, sta, up, down, act_m, act_e, hid_m, hid_e, slope_m, w, act2_m, grad, r3, y3, z3, whole
):
    def body(leading):
        fill3(r3, 0, got_m, 0, 8)
        total = conv(r3, 0, 6, w, 1 if leading else 0, leading)
        if leading:
            act = total * slope_m[rows(2, 6), :]
            act2_m[...] = act.astype(BF16)
            store3(z3, 0, act, 6)
            for a in range(3):
                put_grad(grad, 1, a, outer(hid_m[rows(a, 8), :], r3[rows(0, 8), :]))
                put_grad(grad, 0, a, outer(sta[rows(4 + a, 6), :], z3[rows(0, 6), :]))
        else:
            act, _ = activate(total)
            act2_m[...] = act.astype(BF16)
            fill3(y3, 0, arr, 0, 16)
            whole[rows(0, 4), :] = hid_e[rows(0, 4), :]
            whole[rows(4, 10), :] = hid_m[...]
            whole[rows(14, 4), :] = hid_e[rows(4, 4), :]
            for a in range(3):
                put_grad(grad, 1, a, outer(whole[rows(a, 16), :], y3[...]))
            fill3(z3, 0, act_e, 1, 3)
            fill3(z3, 3, act_m, 0, 10)
            fill3(z3, 13, act_e, 4, 3)
            whole[rows(0, 1), :] = up[1, rows(1, 1), :]
            whole[rows(1, 16), :] = sta[...]
            whole[rows(17, 1), :] = down[1, rows(0, 1), :]
            for a in range(3):
                put_grad(grad, 0, a, outer(whole[rows(a, 16), :], z3[...]))

    by_role(body)


def kernel_d(got_m, got_e, sta, hid_m, hid_e, slope_m, slope_e, grad_in, w, act2_e, grad, r3, z3, h6):
    def body(leading):
        fill3(r3, 0, got_e, 0, 4)
        fill3(r3, 4, got_m, 0, 2)
        fill3(r3, 6, got_m, 6, 2)
        fill3(r3, 8, got_e, 4, 4)
        for half in range(2):
            total = conv(r3, 6 * half, 4, w, 1 if leading else 0, leading)
            if leading:
                if half == 0:
                    slope = jnp.concatenate([slope_e[rows(2, 2), :], slope_m[rows(0, 2), :]], axis=0)
                else:
                    slope = jnp.concatenate([slope_m[rows(8, 2), :], slope_e[rows(4, 2), :]], axis=0)
                act = total * slope
                store3(z3, 4 * half, act, 4)
            else:
                act, _ = activate(total)
            act2_e[rows(4 * half, 4), :] = act.astype(BF16)
        if leading:
            h6[rows(0, 4), :] = hid_e[rows(0, 4), :]
            h6[rows(4, 2), :] = hid_m[rows(0, 2), :]
            h6[rows(6, 2), :] = hid_m[rows(8, 2), :]
            h6[rows(8, 4), :] = hid_e[rows(4, 4), :]
            for a in range(3):
                more = outer(h6[rows(a, 4), :], r3[rows(0, 4), :])
                more = more + outer(h6[rows(6 + a, 4), :], r3[rows(8, 4), :])
                put_grad(grad, 1, a, get_grad(grad_in, 1, a) + more)
                more = outer(sta[rows(a, 4), :], z3[rows(0, 4), :])
                more = more + outer(sta[rows(10 + a, 4), :], z3[rows(4, 4), :])
                put_grad(grad, 0, a, get_grad(grad_in, 0, a) + more)

    by_role(body)


def kernel_e(
    scale, got_e, got_up, got_down, sta, up, down, slope_e, grad_c, grad_d, w, act2_h, send, keep, r3, z3, x2, tot
):
    has_up, has_down = edge_flags()
    core = lax.axis_index("space_2")

    def emit(src, from_at, to_at, width):
        for pair in range(8):
            for dst, side in ((keep, core), (send, 1 - core)):
                first = pl.multiple_of(32 * pair + 8 * side, 8)
                second = pl.multiple_of(32 * pair + 16 + 8 * side, 8)
                val = jnp.concatenate(
                    [
                        src[pl.ds(first, 8), from_at : from_at + width],
                        src[pl.ds(second, 8), from_at : from_at + width],
                    ],
                    axis=0,
                )
                dst[pl.ds(16 * pair, 16), to_at : to_at + width] = (val * scale).astype(dst.dtype)

    def body(leading):
        store3(r3, 0, got_up[...], 2)
        fill3(r3, 2, got_e, 0, 2)
        fill3(r3, 4, got_e, 6, 2)
        store3(r3, 6, got_down[...], 2)
        spot = lax.broadcasted_iota(jnp.int32, (2 * COLS, CH), 0) // COLS
        for half in range(2):
            total = conv(r3, 4 * half, 2, w, 1 if leading else 0, leading)
            if leading:
                act = total * slope_e[rows(6 * half, 2), :]
            else:
                act, _ = activate(total)
            if half == 0:
                act = act * jnp.where(spot == 0, has_up, 1.0)
            else:
                act = act * jnp.where(spot == 1, has_down, 1.0)
            act2_h[rows(2 * half, 2), :] = act.astype(BF16)
        if leading:
            store3(z3, 0, act2_h[rows(1, 2), :], 2)
            x2[rows(0, 1), :] = up[1, rows(1, 1), :]
            x2[rows(1, 2), :] = sta[rows(0, 2), :]
            x2[rows(3, 2), :] = sta[rows(14, 2), :]
            x2[rows(5, 1), :] = down[1, rows(0, 1), :]
            for a in range(3):
                left = jnp.concatenate([x2[rows(a, 1), :], x2[rows(3 + a, 1), :]], axis=0)
                put_grad(tot, 0, a, get_grad(grad_d, 0, a) + outer(left, z3[...]))
            emit(tot, 0, 0, TAPS)
            emit(grad_d, TAPS, TAPS, TAPS)
        else:
            emit(grad_c, 0, 0, 2 * TAPS)

    by_role(body)


def kernel_f(got_m, got_e, act2_m, act2_e, act2_h, w, out, c3):
    def body(leading):
        fill3(c3, 0, act2_h, 0, 2)
        fill3(c3, 2, act2_e, 0, 4)
        fill3(c3, 6, act2_m, 0, 6)
        fill3(c3, 12, act2_e, 4, 4)
        fill3(c3, 16, act2_h, 2, 2)
        for row in (0, 4, 8, 12):
            total = conv(c3, row, 4, w, 0 if leading else 1, leading)
            if row == 0:
                kept = got_e[rows(0, 4), :]
            elif row == 12:
                kept = got_e[rows(4, 4), :]
            else:
                kept = got_m[rows(row - 4, 4), :]
            out[rows(row, 4), :] = (total + kept.astype(F32)).astype(BF16)

    by_role(body)


def call(body, name, outs, scratch, args, row_units, limit=44):
    block = pl.BlockSpec(memory_space=pltpu.VMEM)
    return pl.pallas_call(
        body,
        out_shape=[jax.ShapeDtypeStruct(shape, dtype) for shape, dtype in outs],
        in_specs=[block] * len(args),
        out_specs=[block] * len(outs),
        scratch_shapes=[pltpu.VMEM(shape, dtype) for shape, dtype in scratch],
        compiler_params=pltpu.CompilerParams(vmem_limit_bytes=limit * MIB),
        cost_estimate=pl.CostEstimate(
            flops=int(row_units * 2 * COLS * TAPS * CH),
            bytes_accessed=4 * MIB,
            transcendentals=0,
        ),
        name=name,
    )(*args)


def body(arrivals, stashed, weights):
    arr = arrivals.reshape(-1, CH)
    sta = stashed.reshape(-1, CH)
    w = weights[0, 0]
    tile = arr.shape[0] // COLS
    space = lax.axis_size(SPACE)
    scale = 1.0 / math.sqrt(tile * space * COLS)

    def img(count, dtype=BF16):
        return ((count * COLS, CH), dtype)

    def img3(count):
        return ((count * COLS, 3 * CH), BF16)

    grad_shape = ((CH, 2 * TAPS), F32)

    two = 2 * COLS
    low = jnp.stack([arr[-two:], sta[-two:]])
    high = jnp.stack([arr[:two], sta[:two]])
    ahead = [(i, i + 1) for i in range(space - 1)]
    back = [(j, i) for i, j in ahead]
    up = lax.ppermute(low, SPACE, ahead)
    down = lax.ppermute(high, SPACE, back)

    out_m, act_m, hid_m, slope_m = call(
        kernel_a,
        "first_middle",
        [img(8), img(10), img(10), img(10, F32)],
        [img3(12), img3(12), img3(10)],
        (arr, sta, w),
        28,
    )
    swap = [(0, 1), (1, 0)]
    got_m = lax.ppermute(out_m, "segment", swap)
    out_e, act_e, hid_e, slope_e = call(
        kernel_b,
        "first_edges",
        [img(8), img(8), img(8), img(8, F32)],
        [img3(12), img3(12), img3(12)],
        (arr, sta, up, down, act_m, w),
        24,
    )
    got_e = lax.ppermute(out_e, "segment", swap)
    both = ("segment",) + SPACE
    across_ahead = [((s * space + i), ((1 - s) * space + j)) for s in range(2) for i, j in ahead]
    across_back = [((s * space + i), ((1 - s) * space + j)) for s in range(2) for i, j in back]
    got_up = lax.ppermute(out_e[-two:], both, across_ahead)
    got_down = lax.ppermute(out_e[:two], both, across_back)

    act2_m, grad_c = call(
        kernel_c,
        "second_middle",
        [img(6), grad_shape],
        [img3(8), img3(16), img3(16), img(18)],
        (got_m, arr, sta, up, down, act_m, act_e, hid_m, hid_e, slope_m, w),
        38,
    )
    act2_e, grad_d = call(
        kernel_d,
        "second_edges",
        [img(8), grad_shape],
        [img3(12), img3(8), img(12)],
        (got_m, got_e, sta, hid_m, hid_e, slope_m, slope_e, grad_c, w),
        24,
    )
    act2_h, send, keep = call(
        functools.partial(kernel_e, scale),
        "second_halo",
        [img(4), ((CH // 2, 2 * TAPS), BF16), ((CH // 2, 2 * TAPS), F32)],
        [img3(8), img3(2), img(6), ((CH, TAPS), F32)],
        (got_e, got_up, got_down, sta, up, down, slope_e, grad_c, grad_d, w),
        8,
    )
    (departing,) = call(
        kernel_f,
        "second_out",
        [img(16)],
        [img3(18)],
        (got_m, got_e, act2_m, act2_e, act2_h, w),
        16,
    )

    chips = space // 2
    share = CH // space
    other = lax.ppermute(send, "space_2", swap)
    pieces = (keep + other.astype(F32)).astype(BF16).reshape(chips, share, 2 * TAPS)
    pieces = lax.all_to_all(pieces, ("space_0", "space_1"), 0, 0, tiled=True)
    owned = jnp.sum(pieces.astype(F32), axis=0)
    pairs = [(i, i ^ 3) for i in range(4)]
    partner = lax.ppermute(owned.astype(BF16), ("segment", "mirror"), pairs)
    combined = owned + partner.astype(F32)
    return (
        departing.reshape(arrivals.shape),
        combined.reshape(1, 1, share, 2, 3, 3, CH),
    )


def solution(mesh):
    split = Mesh(
        mesh.devices.reshape(mesh.shape["segment"], 4, 4, 2, mesh.shape["mirror"]),
        ("segment", "space_0", "space_1", "space_2", "mirror"),
    )
    in_specs = (
        P("mirror", "segment", SPACE, None, None),
        P("mirror", "segment", SPACE, None, None),
        P("mirror", "segment", None, None, None, None, None),
    )
    out_specs = (
        P("mirror", "segment", SPACE, None, None),
        P("mirror", "segment", SPACE, None, None, None, None),
    )
    return jax.shard_map(body, mesh=split, in_specs=in_specs, out_specs=out_specs, check_vma=False)
```

```python
import functools
import math

import jax
import jax.numpy as jnp
from jax import lax
from jax.experimental import pallas as pl
from jax.experimental.pallas import tpu as pltpu
from jax.sharding import Mesh
from jax.sharding import PartitionSpec as P

SPACE = ("space_0", "space_1", "space_2")
BF16 = jnp.bfloat16
F32 = jnp.float32
COLS = 128
CH = 256
TAPS = 9 * CH
MIB = 1 << 20


def rows(first, count):
    start = first * COLS
    if not isinstance(start, int):
        start = pl.multiple_of(start, COLS)
    return pl.ds(start, count * COLS)


def repeat(steps, body):
    def step(index, carry):
        body(index)
        return carry

    lax.fori_loop(0, steps, step, 0)


def store3(dst, row, val, count):
    size = count * COLS
    col = lax.broadcasted_iota(jnp.int32, (size, CH), 0) & (COLS - 1)
    val = val.astype(F32)
    left = jnp.where(col == 0, 0.0, pltpu.roll(val, 1, 0))
    right = jnp.where(col == COLS - 1, 0.0, pltpu.roll(val, size - 1, 0))
    where = rows(row, count)
    dst[where, 0:CH] = left.astype(BF16)
    dst[where, CH : 2 * CH] = val.astype(BF16)
    dst[where, 2 * CH :] = right.astype(BF16)


def fill3(dst, row, src, first, count):
    for step in range(0, count, 2):
        size = min(2, count - step)
        store3(dst, row + step, src[rows(first + step, size), :], size)


def conv(src3, first, count, weights, which, transposed):
    total = None
    for a in range(3):
        for b in range(3):
            window = src3[rows(first + a, count), b * CH : (b + 1) * CH]
            if transposed:
                part = lax.dot_general(
                    window,
                    weights[which, 2 - a, 2 - b],
                    (((1,), (1,)), ((), ())),
                    preferred_element_type=F32,
                )
            else:
                part = jnp.dot(window, weights[which, a, b], preferred_element_type=F32)
            total = part if total is None else total + part
    return total


def outer(left, right):
    return lax.dot_general(left, right, (((0,), (0,)), ((), ())), preferred_element_type=F32)


def put_grad(dst, conv_index, a, val):
    for b in range(3):
        at = conv_index * TAPS + (3 * a + b) * CH
        if not isinstance(at, int):
            at = pl.multiple_of(at, CH)
        dst[:, pl.ds(at, CH)] = val[:, (2 - b) * CH : (3 - b) * CH]


def get_grad(src, conv_index, a):
    parts = []
    for b in (2, 1, 0):
        at = conv_index * TAPS + (3 * a + b) * CH
        parts.append(src[:, at : at + CH])
    return jnp.concatenate(parts, axis=1)


def activate(pre):
    sig = jax.nn.sigmoid(pre)
    return pre * sig, sig * (1.0 + pre * (1.0 - sig))


def is_leading():
    return lax.axis_index("segment") == lax.axis_index("mirror")


def by_role(body):
    leading = is_leading()

    @pl.when(leading)
    def _():
        body(True)

    @pl.when(jnp.logical_not(leading))
    def _():
        body(False)


def edge_flags():
    place = lax.axis_index(SPACE)
    count = lax.axis_size(SPACE)
    return (place > 0).astype(F32), (place < count - 1).astype(F32)


def kernel_load(arr_hbm, sta_hbm, w_hbm, low, high, arr, sta, w, sems):
    two = 2 * COLS
    size = arr_hbm.shape[0]
    moves = (
        (arr_hbm.at[pl.ds(size - two, two)], low.at[0]),
        (sta_hbm.at[pl.ds(size - two, two)], low.at[1]),
        (arr_hbm.at[pl.ds(0, two)], high.at[0]),
        (sta_hbm.at[pl.ds(0, two)], high.at[1]),
        (w_hbm.at[0], w.at[0]),
        (sta_hbm, sta),
        (arr_hbm, arr),
        (w_hbm.at[1], w.at[1]),
    )
    copies = [pltpu.make_async_copy(src, dst, sems.at[i]) for i, (src, dst) in enumerate(moves)]
    for copy in copies:
        copy.start()
    for copy in copies:
        copy.wait()


def kernel_a(arr, sta, w, out_m, act_m, hid_m, slope_m, s3, a3, c3):
    def body(leading):
        fill3(s3, 0, sta, 2, 12)
        fill3(a3, 0, arr, 2, 12)

        def inner(step):
            row = 5 * step
            pre = conv(s3, row, 5, w, 0, False)
            hid, slope = activate(pre)
            hid_m[rows(row, 5), :] = hid.astype(BF16)
            slope_m[rows(row, 5), :] = slope
            if leading:
                act, _ = activate(conv(a3, row, 5, w, 0, False))
            else:
                act = conv(a3, row, 5, w, 1, True) * slope
            act_m[rows(row, 5), :] = act.astype(BF16)
            store3(c3, row, act, 5)

        def last(step):
            row = 4 * step
            total = conv(c3, row, 4, w, 1 if leading else 0, not leading)
            out_m[rows(row, 4), :] = (total + arr[rows(4 + row, 4), :].astype(F32)).astype(BF16)

        repeat(2, inner)
        repeat(2, last)

    by_role(body)


def kernel_b(arr, sta, up, down, act_m, w, out_e, act_e, hid_e, slope_e, s3, a3, c3):
    has_up, has_down = edge_flags()

    def body(leading):
        for half in range(2):
            if half == 0:
                store3(s3, 0, up[1], 2)
                fill3(s3, 2, sta, 0, 4)
                store3(a3, 0, up[0], 2)
                fill3(a3, 2, arr, 0, 4)
            else:
                fill3(s3, 6, sta, 12, 4)
                store3(s3, 10, down[1], 2)
                fill3(a3, 6, arr, 12, 4)
                store3(a3, 10, down[0], 2)
            pre = conv(s3, 6 * half, 4, w, 0, False)
            hid, slope = activate(pre)
            spot = lax.broadcasted_iota(jnp.int32, (4 * COLS, CH), 0) // COLS
            if half == 0:
                mask = jnp.where(spot == 0, has_up, 1.0)
            else:
                mask = jnp.where(spot == 3, has_down, 1.0)
            hid_e[rows(4 * half, 4), :] = (hid * mask).astype(BF16)
            slope_e[rows(4 * half, 4), :] = slope
            if leading:
                act, _ = activate(conv(a3, 6 * half, 4, w, 0, False))
            else:
                act = conv(a3, 6 * half, 4, w, 1, True) * slope
            act = act * mask
            act_e[rows(4 * half, 4), :] = act.astype(BF16)
            if half == 0:
                store3(c3, 0, act, 4)
                fill3(c3, 4, act_m, 0, 2)
            else:
                fill3(c3, 6, act_m, 8, 2)
                store3(c3, 8, act, 4)
            total = conv(c3, 6 * half, 4, w, 1 if leading else 0, not leading)
            kept = arr[rows(12 * half, 4), :].astype(F32)
            out_e[rows(4 * half, 4), :] = (total + kept).astype(BF16)

    by_role(body)


def kernel_c(
    got_m, arr, sta, up, down, act_m, act_e, hid_m, hid_e, slope_m, w, act2_m, grad, r3, y3, z3, whole
):
    def body(leading):
        fill3(r3, 0, got_m, 0, 8)
        total = conv(r3, 0, 6, w, 1 if leading else 0, leading)
        if leading:
            act = total * slope_m[rows(2, 6), :]
            act2_m[...] = act.astype(BF16)
            store3(z3, 0, act, 6)
            for a in range(3):
                put_grad(grad, 1, a, outer(hid_m[rows(a, 8), :], r3[rows(0, 8), :]))
                put_grad(grad, 0, a, outer(sta[rows(4 + a, 6), :], z3[rows(0, 6), :]))
        else:
            act, _ = activate(total)
            act2_m[...] = act.astype(BF16)

            def shift_arr(step):
                store3(y3, 2 * step, arr[rows(2 * step, 2), :], 2)

            repeat(8, shift_arr)
            whole[rows(0, 4), :] = hid_e[rows(0, 4), :]
            whole[rows(4, 10), :] = hid_m[...]
            whole[rows(14, 4), :] = hid_e[rows(4, 4), :]

            def second_grad(a):
                put_grad(grad, 1, a, outer(whole[rows(a, 16), :], y3[...]))

            def first_grad(a):
                put_grad(grad, 0, a, outer(whole[rows(a, 16), :], z3[...]))

            repeat(3, second_grad)
            fill3(z3, 0, act_e, 1, 3)
            fill3(z3, 3, act_m, 0, 10)
            fill3(z3, 13, act_e, 4, 3)
            whole[rows(0, 1), :] = up[1, rows(1, 1), :]
            whole[rows(1, 16), :] = sta[...]
            whole[rows(17, 1), :] = down[1, rows(0, 1), :]
            repeat(3, first_grad)

    by_role(body)


def kernel_d(got_m, got_e, sta, hid_m, hid_e, slope_m, slope_e, grad_in, w, act2_e, grad, r3, z3, h6):
    def body(leading):
        fill3(r3, 0, got_e, 0, 4)
        fill3(r3, 4, got_m, 0, 2)
        fill3(r3, 6, got_m, 6, 2)
        fill3(r3, 8, got_e, 4, 4)
        for half in range(2):
            total = conv(r3, 6 * half, 4, w, 1 if leading else 0, leading)
            if leading:
                if half == 0:
                    slope = jnp.concatenate([slope_e[rows(2, 2), :], slope_m[rows(0, 2), :]], axis=0)
                else:
                    slope = jnp.concatenate([slope_m[rows(8, 2), :], slope_e[rows(4, 2), :]], axis=0)
                act = total * slope
                store3(z3, 4 * half, act, 4)
            else:
                act, _ = activate(total)
            act2_e[rows(4 * half, 4), :] = act.astype(BF16)
        if leading:
            h6[rows(0, 4), :] = hid_e[rows(0, 4), :]
            h6[rows(4, 2), :] = hid_m[rows(0, 2), :]
            h6[rows(6, 2), :] = hid_m[rows(8, 2), :]
            h6[rows(8, 4), :] = hid_e[rows(4, 4), :]
            for a in range(3):
                more = outer(h6[rows(a, 4), :], r3[rows(0, 4), :])
                more = more + outer(h6[rows(6 + a, 4), :], r3[rows(8, 4), :])
                put_grad(grad, 1, a, get_grad(grad_in, 1, a) + more)
                more = outer(sta[rows(a, 4), :], z3[rows(0, 4), :])
                more = more + outer(sta[rows(10 + a, 4), :], z3[rows(4, 4), :])
                put_grad(grad, 0, a, get_grad(grad_in, 0, a) + more)

    by_role(body)


def kernel_e(
    scale, got_e, got_up, got_down, sta, up, down, slope_e, grad_c, grad_d, w, act2_h, send, keep, r3, z3, x2, tot
):
    has_up, has_down = edge_flags()
    core = lax.axis_index("space_2")

    def emit(src, from_at, to_at, width):
        for pair in range(8):
            for dst, side in ((keep, core), (send, 1 - core)):
                first = pl.multiple_of(32 * pair + 8 * side, 8)
                second = pl.multiple_of(32 * pair + 16 + 8 * side, 8)
                val = jnp.concatenate(
                    [
                        src[pl.ds(first, 8), from_at : from_at + width],
                        src[pl.ds(second, 8), from_at : from_at + width],
                    ],
                    axis=0,
                )
                dst[pl.ds(16 * pair, 16), to_at : to_at + width] = (val * scale).astype(dst.dtype)

    def body(leading):
        store3(r3, 0, got_up[...], 2)
        fill3(r3, 2, got_e, 0, 2)
        fill3(r3, 4, got_e, 6, 2)
        store3(r3, 6, got_down[...], 2)
        spot = lax.broadcasted_iota(jnp.int32, (2 * COLS, CH), 0) // COLS
        for half in range(2):
            total = conv(r3, 4 * half, 2, w, 1 if leading else 0, leading)
            if leading:
                act = total * slope_e[rows(6 * half, 2), :]
            else:
                act, _ = activate(total)
            if half == 0:
                act = act * jnp.where(spot == 0, has_up, 1.0)
            else:
                act = act * jnp.where(spot == 1, has_down, 1.0)
            act2_h[rows(2 * half, 2), :] = act.astype(BF16)
        if leading:
            store3(z3, 0, act2_h[rows(1, 2), :], 2)
            x2[rows(0, 1), :] = up[1, rows(1, 1), :]
            x2[rows(1, 2), :] = sta[rows(0, 2), :]
            x2[rows(3, 2), :] = sta[rows(14, 2), :]
            x2[rows(5, 1), :] = down[1, rows(0, 1), :]
            for a in range(3):
                left = jnp.concatenate([x2[rows(a, 1), :], x2[rows(3 + a, 1), :]], axis=0)
                put_grad(tot, 0, a, get_grad(grad_d, 0, a) + outer(left, z3[...]))
            emit(tot, 0, 0, TAPS)
            emit(grad_d, TAPS, TAPS, TAPS)
        else:
            emit(grad_c, 0, 0, 2 * TAPS)

    by_role(body)


def kernel_f(got_m, got_e, act2_m, act2_e, act2_h, w, out, c3, kept):
    def body(leading):
        fill3(c3, 0, act2_h, 0, 2)
        fill3(c3, 2, act2_e, 0, 4)
        fill3(c3, 6, act2_m, 0, 6)
        fill3(c3, 12, act2_e, 4, 4)
        fill3(c3, 16, act2_h, 2, 2)
        kept[rows(0, 4), :] = got_e[rows(0, 4), :]
        kept[rows(4, 8), :] = got_m[...]
        kept[rows(12, 4), :] = got_e[rows(4, 4), :]

        def block(step):
            row = 4 * step
            total = conv(c3, row, 4, w, 0 if leading else 1, leading)
            out[rows(row, 4), :] = (total + kept[rows(row, 4), :].astype(F32)).astype(BF16)

        repeat(4, block)

    by_role(body)


def call(body, name, outs, scratch, args, row_units, limit=18):
    block = pl.BlockSpec(memory_space=pltpu.VMEM)
    return pl.pallas_call(
        body,
        out_shape=[jax.ShapeDtypeStruct(shape, dtype) for shape, dtype in outs],
        in_specs=[block] * len(args),
        out_specs=[block] * len(outs),
        scratch_shapes=[pltpu.VMEM(shape, dtype) for shape, dtype in scratch],
        compiler_params=pltpu.CompilerParams(vmem_limit_bytes=limit * MIB),
        cost_estimate=pl.CostEstimate(
            flops=int(row_units * 2 * COLS * TAPS * CH),
            bytes_accessed=4 * MIB,
            transcendentals=0,
        ),
        name=name,
    )(*args)


def body(arrivals, stashed, weights):
    arr = arrivals.reshape(-1, CH)
    sta = stashed.reshape(-1, CH)
    w = weights[0, 0]
    tile = arr.shape[0] // COLS
    space = lax.axis_size(SPACE)
    scale = 1.0 / math.sqrt(tile * space * COLS)

    def img(count, dtype=BF16):
        return ((count * COLS, CH), dtype)

    def img3(count):
        return ((count * COLS, 3 * CH), BF16)

    grad_shape = ((CH, 2 * TAPS), F32)

    two = 2 * COLS
    vmem = pl.BlockSpec(memory_space=pltpu.VMEM)
    edge = jax.ShapeDtypeStruct((2, two, CH), BF16)
    low, high, arr, sta, w = pl.pallas_call(
        kernel_load,
        out_shape=[edge, edge] + [jax.ShapeDtypeStruct(v.shape, BF16) for v in (arr, sta, w)],
        in_specs=[pl.BlockSpec(memory_space=pltpu.HBM)] * 3,
        out_specs=[vmem] * 5,
        scratch_shapes=[pltpu.SemaphoreType.DMA((8,))],
        compiler_params=pltpu.CompilerParams(vmem_limit_bytes=8 * MIB),
        name="load",
    )(arr, sta, w)
    ahead = [(i, i + 1) for i in range(space - 1)]
    back = [(j, i) for i, j in ahead]
    up = lax.ppermute(low, SPACE, ahead)
    down = lax.ppermute(high, SPACE, back)

    out_m, act_m, hid_m, slope_m = call(
        kernel_a,
        "first_middle",
        [img(8), img(10), img(10), img(10, F32)],
        [img3(12), img3(12), img3(10)],
        (arr, sta, w),
        28,
    )
    swap = [(0, 1), (1, 0)]
    got_m = lax.ppermute(out_m, "segment", swap)
    out_e, act_e, hid_e, slope_e = call(
        kernel_b,
        "first_edges",
        [img(8), img(8), img(8), img(8, F32)],
        [img3(12), img3(12), img3(12)],
        (arr, sta, up, down, act_m, w),
        24,
    )
    got_e = lax.ppermute(out_e, "segment", swap)
    both = ("segment",) + SPACE
    across_ahead = [((s * space + i), ((1 - s) * space + j)) for s in range(2) for i, j in ahead]
    across_back = [((s * space + i), ((1 - s) * space + j)) for s in range(2) for i, j in back]

    tail, head = out_e[-two:], out_e[:two]
    act2_m, grad_c = call(
        kernel_c,
        "second_middle",
        [img(6), grad_shape],
        [img3(8), img3(16), img3(16), img(18)],
        (got_m, arr, sta, up, down, act_m, act_e, hid_m, hid_e, slope_m, w),
        38,
    )
    act2_m, tail, head = lax.optimization_barrier((act2_m, tail, head))
    got_up = lax.ppermute(tail, both, across_ahead)
    got_down = lax.ppermute(head, both, across_back)
    act2_e, grad_d = call(
        kernel_d,
        "second_edges",
        [img(8), grad_shape],
        [img3(12), img3(8), img(12)],
        (got_m, got_e, sta, hid_m, hid_e, slope_m, slope_e, grad_c, w),
        24,
    )
    act2_h, send, keep = call(
        functools.partial(kernel_e, scale),
        "second_halo",
        [img(4), ((CH // 2, 2 * TAPS), BF16), ((CH // 2, 2 * TAPS), F32)],
        [img3(8), img3(2), img(6), ((CH, TAPS), F32)],
        (got_e, got_up, got_down, sta, up, down, slope_e, grad_c, grad_d, w),
        8,
    )
    (departing,) = call(
        kernel_f,
        "second_out",
        [img(16)],
        [img3(18), img(16)],
        (got_m, got_e, act2_m, act2_e, act2_h, w),
        16,
    )

    chips = space // 2
    share = CH // space
    other = lax.ppermute(send, "space_2", swap)
    pieces = (keep + other.astype(F32)).astype(BF16).reshape(chips, share, 2 * TAPS)
    pieces = lax.all_to_all(pieces, ("space_0", "space_1"), 0, 0, tiled=True)
    owned = jnp.sum(pieces.astype(F32), axis=0)
    owned, departing = lax.optimization_barrier((owned, departing))
    pairs = [(i, i ^ 3) for i in range(4)]
    partner = lax.ppermute(owned.astype(BF16), ("segment", "mirror"), pairs)
    combined = owned + partner.astype(F32)
    return (
        departing.reshape(arrivals.shape),
        combined.reshape(1, 1, share, 2, 3, 3, CH),
    )


def solution(mesh):
    split = Mesh(
        mesh.devices.reshape(mesh.shape["segment"], 4, 4, 2, mesh.shape["mirror"]),
        ("segment", "space_0", "space_1", "space_2", "mirror"),
    )
    in_specs = (
        P("mirror", "segment", SPACE, None, None),
        P("mirror", "segment", SPACE, None, None),
        P("mirror", "segment", None, None, None, None, None),
    )
    out_specs = (
        P("mirror", "segment", SPACE, None, None),
        P("mirror", "segment", SPACE, None, None, None, None),
    )
    return jax.shard_map(body, mesh=split, in_specs=in_specs, out_specs=out_specs, check_vma=False)
```

```python
import functools
import math

import jax
import jax.numpy as jnp
from jax import lax
from jax.experimental import pallas as pl
from jax.experimental.pallas import tpu as pltpu
from jax.sharding import Mesh
from jax.sharding import PartitionSpec as P

SPACE = ("space_0", "space_1", "space_2")
BF16 = jnp.bfloat16
F32 = jnp.float32
COLS = 128
CH = 256
TAPS = 9 * CH
MIB = 1 << 20
LIMIT_A = 49


def rows(first, count):
    start = first * COLS
    if not isinstance(start, int):
        start = pl.multiple_of(start, COLS)
    return pl.ds(start, count * COLS)


def repeat(steps, body):
    def step(index, carry):
        body(index)
        return carry

    lax.fori_loop(0, steps, step, 0)


def store3(dst, row, val, count):
    size = count * COLS
    col = lax.broadcasted_iota(jnp.int32, (size, CH), 0) & (COLS - 1)
    val = val.astype(F32)
    left = jnp.where(col == 0, 0.0, pltpu.roll(val, 1, 0))
    right = jnp.where(col == COLS - 1, 0.0, pltpu.roll(val, size - 1, 0))
    where = rows(row, count)
    dst[where, 0:CH] = left.astype(BF16)
    dst[where, CH : 2 * CH] = val.astype(BF16)
    dst[where, 2 * CH :] = right.astype(BF16)


def fill3(dst, row, src, first, count):
    for step in range(0, count, 2):
        size = min(2, count - step)
        store3(dst, row + step, src[rows(first + step, size), :], size)


def conv(src3, first, count, weights, which, transposed):
    total = None
    for a in range(3):
        for b in range(3):
            window = src3[rows(first + a, count), b * CH : (b + 1) * CH]
            if transposed:
                part = lax.dot_general(
                    window,
                    weights[which, 2 - a, 2 - b],
                    (((1,), (1,)), ((), ())),
                    preferred_element_type=F32,
                )
            else:
                part = jnp.dot(window, weights[which, a, b], preferred_element_type=F32)
            total = part if total is None else total + part
    return total


def outer(left, right):
    return lax.dot_general(left, right, (((0,), (0,)), ((), ())), preferred_element_type=F32)


def put_grad(dst, conv_index, a, val):
    for b in range(3):
        at = conv_index * TAPS + (3 * a + b) * CH
        if not isinstance(at, int):
            at = pl.multiple_of(at, CH)
        dst[:, pl.ds(at, CH)] = val[:, (2 - b) * CH : (3 - b) * CH]


def get_grad(src, conv_index, a):
    parts = []
    for b in (2, 1, 0):
        at = conv_index * TAPS + (3 * a + b) * CH
        parts.append(src[:, at : at + CH])
    return jnp.concatenate(parts, axis=1)


def activate(pre):
    sig = jax.nn.sigmoid(pre)
    return pre * sig, sig * (1.0 + pre * (1.0 - sig))


def is_leading():
    return lax.axis_index("segment") == lax.axis_index("mirror")


def by_role(body):
    leading = is_leading()

    @pl.when(leading)
    def _():
        body(True)

    @pl.when(jnp.logical_not(leading))
    def _():
        body(False)


def edge_flags():
    place = lax.axis_index(SPACE)
    count = lax.axis_size(SPACE)
    return (place > 0).astype(F32), (place < count - 1).astype(F32)


def kernel_a(
    arr_hbm, sta_hbm, w_hbm, out_m, act_m, hid_m, slope_m, low, high, arr, sta, s3, a3, c3, w, sems
):
    two = 2 * COLS
    size = arr_hbm.shape[0]
    moves = (
        (sta_hbm, sta),
        (arr_hbm, arr),
        (w_hbm.at[0], w.at[0]),
        (w_hbm.at[1], w.at[1]),
        (arr_hbm.at[pl.ds(size - two, two)], low.at[0]),
        (sta_hbm.at[pl.ds(size - two, two)], low.at[1]),
        (arr_hbm.at[pl.ds(0, two)], high.at[0]),
        (sta_hbm.at[pl.ds(0, two)], high.at[1]),
    )
    copies = [pltpu.make_async_copy(src, dst, sems.at[i]) for i, (src, dst) in enumerate(moves)]
    for copy in copies:
        copy.start()
    copies[0].wait()
    fill3(s3, 0, sta, 2, 12)
    copies[1].wait()
    fill3(a3, 0, arr, 2, 12)
    for copy in copies[2:]:
        copy.wait()

    def body(leading):

        def inner(step):
            row = 5 * step
            pre = conv(s3, row, 5, w, 0, False)
            hid, slope = activate(pre)
            hid_m[rows(row, 5), :] = hid.astype(BF16)
            slope_m[rows(row, 5), :] = slope
            if leading:
                act, _ = activate(conv(a3, row, 5, w, 0, False))
            else:
                act = conv(a3, row, 5, w, 1, True) * slope
            act_m[rows(row, 5), :] = act.astype(BF16)
            store3(c3, row, act, 5)

        def last(step):
            row = 4 * step
            total = conv(c3, row, 4, w, 1 if leading else 0, not leading)
            out_m[rows(row, 4), :] = (total + arr[rows(4 + row, 4), :].astype(F32)).astype(BF16)

        for step in range(2):
            inner(step)
        for step in range(2):
            last(step)

    by_role(body)


def kernel_b(arr, sta, up, down, act_m, w, out_e, act_e, hid_e, slope_e, s3, a3, c3):
    has_up, has_down = edge_flags()

    def body(leading):
        for half in range(2):
            if half == 0:
                store3(s3, 0, up[1], 2)
                fill3(s3, 2, sta, 0, 4)
                store3(a3, 0, up[0], 2)
                fill3(a3, 2, arr, 0, 4)
            else:
                fill3(s3, 6, sta, 12, 4)
                store3(s3, 10, down[1], 2)
                fill3(a3, 6, arr, 12, 4)
                store3(a3, 10, down[0], 2)
            pre = conv(s3, 6 * half, 4, w, 0, False)
            hid, slope = activate(pre)
            spot = lax.broadcasted_iota(jnp.int32, (4 * COLS, CH), 0) // COLS
            if half == 0:
                mask = jnp.where(spot == 0, has_up, 1.0)
            else:
                mask = jnp.where(spot == 3, has_down, 1.0)
            hid_e[rows(4 * half, 4), :] = (hid * mask).astype(BF16)
            slope_e[rows(4 * half, 4), :] = slope
            if leading:
                act, _ = activate(conv(a3, 6 * half, 4, w, 0, False))
            else:
                act = conv(a3, 6 * half, 4, w, 1, True) * slope
            act = act * mask
            act_e[rows(4 * half, 4), :] = act.astype(BF16)
            if half == 0:
                store3(c3, 0, act, 4)
                fill3(c3, 4, act_m, 0, 2)
            else:
                fill3(c3, 6, act_m, 8, 2)
                store3(c3, 8, act, 4)
            total = conv(c3, 6 * half, 4, w, 1 if leading else 0, not leading)
            kept = arr[rows(12 * half, 4), :].astype(F32)
            out_e[rows(4 * half, 4), :] = (total + kept).astype(BF16)

    by_role(body)


def kernel_c(
    got_m, arr, sta, up, down, act_m, act_e, hid_m, hid_e, slope_m, w, act2_m, grad, r3, y3, z3, whole
):
    def body(leading):
        fill3(r3, 0, got_m, 0, 8)
        total = conv(r3, 0, 6, w, 1 if leading else 0, leading)
        if leading:
            act = total * slope_m[rows(2, 6), :]
            act2_m[...] = act.astype(BF16)
            store3(z3, 0, act, 6)
            for a in range(3):
                put_grad(grad, 1, a, outer(hid_m[rows(a, 8), :], r3[rows(0, 8), :]))
                put_grad(grad, 0, a, outer(sta[rows(4 + a, 6), :], z3[rows(0, 6), :]))
        else:
            act, _ = activate(total)
            act2_m[...] = act.astype(BF16)

            def shift_arr(step):
                store3(y3, 2 * step, arr[rows(2 * step, 2), :], 2)

            repeat(8, shift_arr)
            whole[rows(0, 4), :] = hid_e[rows(0, 4), :]
            whole[rows(4, 10), :] = hid_m[...]
            whole[rows(14, 4), :] = hid_e[rows(4, 4), :]

            def second_grad(a):
                put_grad(grad, 1, a, outer(whole[rows(a, 16), :], y3[...]))

            def first_grad(a):
                put_grad(grad, 0, a, outer(whole[rows(a, 16), :], z3[...]))

            repeat(3, second_grad)
            fill3(z3, 0, act_e, 1, 3)
            fill3(z3, 3, act_m, 0, 10)
            fill3(z3, 13, act_e, 4, 3)
            whole[rows(0, 1), :] = up[1, rows(1, 1), :]
            whole[rows(1, 16), :] = sta[...]
            whole[rows(17, 1), :] = down[1, rows(0, 1), :]
            repeat(3, first_grad)

    by_role(body)


def kernel_d(got_m, got_e, sta, hid_m, hid_e, slope_m, slope_e, grad_in, w, act2_e, grad, r3, z3, h6):
    def body(leading):
        fill3(r3, 0, got_e, 0, 4)
        fill3(r3, 4, got_m, 0, 2)
        fill3(r3, 6, got_m, 6, 2)
        fill3(r3, 8, got_e, 4, 4)
        for half in range(2):
            total = conv(r3, 6 * half, 4, w, 1 if leading else 0, leading)
            if leading:
                if half == 0:
                    slope = jnp.concatenate([slope_e[rows(2, 2), :], slope_m[rows(0, 2), :]], axis=0)
                else:
                    slope = jnp.concatenate([slope_m[rows(8, 2), :], slope_e[rows(4, 2), :]], axis=0)
                act = total * slope
                store3(z3, 4 * half, act, 4)
            else:
                act, _ = activate(total)
            act2_e[rows(4 * half, 4), :] = act.astype(BF16)
        if leading:
            h6[rows(0, 4), :] = hid_e[rows(0, 4), :]
            h6[rows(4, 2), :] = hid_m[rows(0, 2), :]
            h6[rows(6, 2), :] = hid_m[rows(8, 2), :]
            h6[rows(8, 4), :] = hid_e[rows(4, 4), :]
            for a in range(3):
                more = outer(h6[rows(a, 4), :], r3[rows(0, 4), :])
                more = more + outer(h6[rows(6 + a, 4), :], r3[rows(8, 4), :])
                put_grad(grad, 1, a, get_grad(grad_in, 1, a) + more)
                more = outer(sta[rows(a, 4), :], z3[rows(0, 4), :])
                more = more + outer(sta[rows(10 + a, 4), :], z3[rows(4, 4), :])
                put_grad(grad, 0, a, get_grad(grad_in, 0, a) + more)

    by_role(body)


def kernel_e(
    scale, got_e, got_up, got_down, sta, up, down, slope_e, grad_c, grad_d, w, act2_h, send, keep, r3, z3, x2, tot
):
    has_up, has_down = edge_flags()
    core = lax.axis_index("space_2")

    def emit(src, from_at, to_at, width):
        for pair in range(8):
            for dst, side in ((keep, core), (send, 1 - core)):
                first = pl.multiple_of(32 * pair + 8 * side, 8)
                second = pl.multiple_of(32 * pair + 16 + 8 * side, 8)
                val = jnp.concatenate(
                    [
                        src[pl.ds(first, 8), from_at : from_at + width],
                        src[pl.ds(second, 8), from_at : from_at + width],
                    ],
                    axis=0,
                )
                dst[pl.ds(16 * pair, 16), to_at : to_at + width] = (val * scale).astype(dst.dtype)

    def body(leading):
        store3(r3, 0, got_up[...], 2)
        fill3(r3, 2, got_e, 0, 2)
        fill3(r3, 4, got_e, 6, 2)
        store3(r3, 6, got_down[...], 2)
        spot = lax.broadcasted_iota(jnp.int32, (2 * COLS, CH), 0) // COLS
        for half in range(2):
            total = conv(r3, 4 * half, 2, w, 1 if leading else 0, leading)
            if leading:
                act = total * slope_e[rows(6 * half, 2), :]
            else:
                act, _ = activate(total)
            if half == 0:
                act = act * jnp.where(spot == 0, has_up, 1.0)
            else:
                act = act * jnp.where(spot == 1, has_down, 1.0)
            act2_h[rows(2 * half, 2), :] = act.astype(BF16)
        if leading:
            store3(z3, 0, act2_h[rows(1, 2), :], 2)
            x2[rows(0, 1), :] = up[1, rows(1, 1), :]
            x2[rows(1, 2), :] = sta[rows(0, 2), :]
            x2[rows(3, 2), :] = sta[rows(14, 2), :]
            x2[rows(5, 1), :] = down[1, rows(0, 1), :]
            for a in range(3):
                left = jnp.concatenate([x2[rows(a, 1), :], x2[rows(3 + a, 1), :]], axis=0)
                put_grad(tot, 0, a, get_grad(grad_d, 0, a) + outer(left, z3[...]))
            emit(tot, 0, 0, TAPS)
            emit(grad_d, TAPS, TAPS, TAPS)
        else:
            emit(grad_c, 0, 0, 2 * TAPS)

    by_role(body)


def kernel_f(got_m, got_e, act2_m, act2_e, act2_h, w, out, c3, kept):
    def body(leading):
        fill3(c3, 0, act2_h, 0, 2)
        fill3(c3, 2, act2_e, 0, 4)
        fill3(c3, 6, act2_m, 0, 6)
        fill3(c3, 12, act2_e, 4, 4)
        fill3(c3, 16, act2_h, 2, 2)
        kept[rows(0, 4), :] = got_e[rows(0, 4), :]
        kept[rows(4, 8), :] = got_m[...]
        kept[rows(12, 4), :] = got_e[rows(4, 4), :]

        def block(step):
            row = 4 * step
            total = conv(c3, row, 4, w, 0 if leading else 1, leading)
            out[rows(row, 4), :] = (total + kept[rows(row, 4), :].astype(F32)).astype(BF16)

        repeat(4, block)

    by_role(body)


def call(body, name, outs, scratch, args, row_units, limit=18, space=pltpu.VMEM, sems=0):
    block = pl.BlockSpec(memory_space=pltpu.VMEM)
    semaphores = [pltpu.SemaphoreType.DMA((sems,))] if sems else []
    return pl.pallas_call(
        body,
        out_shape=[jax.ShapeDtypeStruct(shape, dtype) for shape, dtype in outs],
        in_specs=[pl.BlockSpec(memory_space=space)] * len(args),
        out_specs=[block] * len(outs),
        scratch_shapes=[pltpu.VMEM(shape, dtype) for shape, dtype in scratch] + semaphores,
        compiler_params=pltpu.CompilerParams(vmem_limit_bytes=limit * MIB),
        cost_estimate=pl.CostEstimate(
            flops=int(row_units * 2 * COLS * TAPS * CH),
            bytes_accessed=4 * MIB,
            transcendentals=0,
        ),
        name=name,
    )(*args)


def body(arrivals, stashed, weights):
    arr = arrivals.reshape(-1, CH)
    sta = stashed.reshape(-1, CH)
    w = weights[0, 0]
    tile = arr.shape[0] // COLS
    space = lax.axis_size(SPACE)
    scale = 1.0 / math.sqrt(tile * space * COLS)

    def img(count, dtype=BF16):
        return ((count * COLS, CH), dtype)

    def img3(count):
        return ((count * COLS, 3 * CH), BF16)

    grad_shape = ((CH, 2 * TAPS), F32)

    two = 2 * COLS
    edge = ((2, two, CH), BF16)
    out_m, act_m, hid_m, slope_m, low, high, arr, sta = call(
        kernel_a,
        "first_middle",
        [img(8), img(10), img(10), img(10, F32), edge, edge, img(16), img(16)],
        [img3(12), img3(12), img3(10), (w.shape, BF16)],
        (arr, sta, w),
        28,
        limit=LIMIT_A,
        space=pltpu.HBM,
        sems=8,
    )
    ahead = [(i, i + 1) for i in range(space - 1)]
    back = [(j, i) for i, j in ahead]
    swap = [(0, 1), (1, 0)]
    got_m = lax.ppermute(out_m, "segment", swap)
    act_m, low, high = lax.optimization_barrier((act_m, low, high))
    up = lax.ppermute(low, SPACE, ahead)
    down = lax.ppermute(high, SPACE, back)
    out_e, act_e, hid_e, slope_e = call(
        kernel_b,
        "first_edges",
        [img(8), img(8), img(8), img(8, F32)],
        [img3(12), img3(12), img3(12)],
        (arr, sta, up, down, act_m, w),
        24,
    )
    got_e = lax.ppermute(out_e, "segment", swap)
    act2_m, grad_c = call(
        kernel_c,
        "second_middle",
        [img(6), grad_shape],
        [img3(8), img3(16), img3(16), img(18)],
        (got_m, arr, sta, up, down, act_m, act_e, hid_m, hid_e, slope_m, w),
        38,
    )
    got_up = lax.ppermute(got_e[-two:], SPACE, ahead)
    got_down = lax.ppermute(got_e[:two], SPACE, back)
    act2_e, grad_d = call(
        kernel_d,
        "second_edges",
        [img(8), grad_shape],
        [img3(12), img3(8), img(12)],
        (got_m, got_e, sta, hid_m, hid_e, slope_m, slope_e, grad_c, w),
        24,
    )
    act2_h, send, keep = call(
        functools.partial(kernel_e, scale),
        "second_halo",
        [img(4), ((CH // 2, 2 * TAPS), BF16), ((CH // 2, 2 * TAPS), F32)],
        [img3(8), img3(2), img(6), ((CH, TAPS), F32)],
        (got_e, got_up, got_down, sta, up, down, slope_e, grad_c, grad_d, w),
        8,
    )
    (departing,) = call(
        kernel_f,
        "second_out",
        [img(16)],
        [img3(18), img(16)],
        (got_m, got_e, act2_m, act2_e, act2_h, w),
        16,
    )

    chips = space // 2
    share = CH // space
    other = lax.ppermute(send, "space_2", swap)
    pieces = (keep + other.astype(F32)).astype(BF16).reshape(chips, share, 2 * TAPS)
    pieces = lax.all_to_all(pieces, ("space_0", "space_1"), 0, 0, tiled=True)
    owned = jnp.sum(pieces.astype(F32), axis=0)
    owned, departing = lax.optimization_barrier((owned, departing))
    pairs = [(i, i ^ 3) for i in range(4)]
    partner = lax.ppermute(owned.astype(BF16), ("segment", "mirror"), pairs)
    combined = owned + partner.astype(F32)
    return (
        departing.reshape(arrivals.shape),
        combined.reshape(1, 1, share, 2, 3, 3, CH),
    )


def solution(mesh):
    split = Mesh(
        mesh.devices.reshape(mesh.shape["segment"], 4, 4, 2, mesh.shape["mirror"]),
        ("segment", "space_0", "space_1", "space_2", "mirror"),
    )
    in_specs = (
        P("mirror", "segment", SPACE, None, None),
        P("mirror", "segment", SPACE, None, None),
        P("mirror", "segment", None, None, None, None, None),
    )
    out_specs = (
        P("mirror", "segment", SPACE, None, None),
        P("mirror", "segment", SPACE, None, None, None, None),
    )
    return jax.shard_map(body, mesh=split, in_specs=in_specs, out_specs=out_specs, check_vma=False)
```

```python
import functools
import math

import jax
import jax.numpy as jnp
from jax import lax
from jax.experimental import pallas as pl
from jax.experimental.pallas import tpu as pltpu
from jax.sharding import Mesh
from jax.sharding import PartitionSpec as P

SPACE = ("space_0", "space_1", "space_2")
BF16 = jnp.bfloat16
F32 = jnp.float32
COLS = 128
CH = 256
TAPS = 9 * CH
MIB = 1 << 20
LIMIT_A = 50


def rows(first, count):
    start = first * COLS
    if not isinstance(start, int):
        start = pl.multiple_of(start, COLS)
    return pl.ds(start, count * COLS)


def repeat(steps, body):
    def step(index, carry):
        body(index)
        return carry

    lax.fori_loop(0, steps, step, 0)


def store3(dst, row, val, count):
    size = count * COLS
    col = lax.broadcasted_iota(jnp.int32, (size, CH), 0) & (COLS - 1)
    val = val.astype(F32)
    left = jnp.where(col == 0, 0.0, pltpu.roll(val, 1, 0))
    right = jnp.where(col == COLS - 1, 0.0, pltpu.roll(val, size - 1, 0))
    where = rows(row, count)
    dst[where, 0:CH] = left.astype(BF16)
    dst[where, CH : 2 * CH] = val.astype(BF16)
    dst[where, 2 * CH :] = right.astype(BF16)


def fill3(dst, row, src, first, count):
    for step in range(0, count, 2):
        size = min(2, count - step)
        store3(dst, row + step, src[rows(first + step, size), :], size)


def conv(src3, first, count, weights, which, transposed):
    total = None
    for a in range(3):
        for b in range(3):
            window = src3[rows(first + a, count), b * CH : (b + 1) * CH]
            if transposed:
                part = lax.dot_general(
                    window,
                    weights[which, 2 - a, 2 - b],
                    (((1,), (1,)), ((), ())),
                    preferred_element_type=F32,
                )
            else:
                part = jnp.dot(window, weights[which, a, b], preferred_element_type=F32)
            total = part if total is None else total + part
    return total


def outer(left, right):
    return lax.dot_general(left, right, (((0,), (0,)), ((), ())), preferred_element_type=F32)


def put_grad(dst, conv_index, a, val):
    for b in range(3):
        at = conv_index * TAPS + (3 * a + b) * CH
        if not isinstance(at, int):
            at = pl.multiple_of(at, CH)
        dst[:, pl.ds(at, CH)] = val[:, (2 - b) * CH : (3 - b) * CH]


def get_grad(src, conv_index, a):
    parts = []
    for b in (2, 1, 0):
        at = conv_index * TAPS + (3 * a + b) * CH
        parts.append(src[:, at : at + CH])
    return jnp.concatenate(parts, axis=1)


def activate(pre):
    sig = jax.nn.sigmoid(pre)
    return pre * sig, sig * (1.0 + pre * (1.0 - sig))


def is_leading():
    return lax.axis_index("segment") == lax.axis_index("mirror")


def by_role(body):
    leading = is_leading()

    @pl.when(leading)
    def _():
        body(True)

    @pl.when(jnp.logical_not(leading))
    def _():
        body(False)


def edge_flags():
    place = lax.axis_index(SPACE)
    count = lax.axis_size(SPACE)
    return (place > 0).astype(F32), (place < count - 1).astype(F32)


def kernel_a(
    arr_hbm, sta_hbm, w_hbm, out_m, act_m, hid_m, slope_m, low, high, sta, s3, a3, c3, w, arr, steep, sems
):
    two = 2 * COLS
    size = arr_hbm.shape[0]
    moves = (
        (sta_hbm, sta),
        (w_hbm.at[0], w.at[0]),
        (arr_hbm, arr),
        (w_hbm.at[1], w.at[1]),
        (arr_hbm.at[pl.ds(size - two, two)], low.at[0]),
        (sta_hbm.at[pl.ds(size - two, two)], low.at[1]),
        (arr_hbm.at[pl.ds(0, two)], high.at[0]),
        (sta_hbm.at[pl.ds(0, two)], high.at[1]),
    )
    copies = [pltpu.make_async_copy(src, dst, sems.at[i]) for i, (src, dst) in enumerate(moves)]
    for copy in copies:
        copy.start()
    copies[0].wait()
    fill3(s3, 0, sta, 2, 12)
    copies[1].wait()
    copies[2].wait()

    def body(leading):
        fill3(a3, 0, arr, 2, 12)
        for row in (0, 5):
            pre = conv(s3, row, 5, w, 0, False)
            hid, slope = activate(pre)
            hid_m[rows(row, 5), :] = hid.astype(BF16)
            if leading:
                slope_m[rows(row, 5), :] = slope.astype(BF16)
            else:
                steep[rows(row, 5), :] = slope
        for copy in copies[3:]:
            copy.wait()
        for row in (0, 5):
            if leading:
                act, _ = activate(conv(a3, row, 5, w, 0, False))
            else:
                act = conv(a3, row, 5, w, 1, True) * steep[rows(row, 5), :]
            act_m[rows(row, 5), :] = act.astype(BF16)
            store3(c3, row, act, 5)
        for row in (0, 4):
            total = conv(c3, row, 4, w, 1 if leading else 0, not leading)
            out_m[rows(row, 4), :] = (total + arr[rows(4 + row, 4), :].astype(F32)).astype(BF16)

    by_role(body)


def kernel_b(arr, sta, up, down, act_m, w, out_e, act_e, hid_e, slope_e, s3, a3, c3):
    has_up, has_down = edge_flags()

    def body(leading):
        for half in range(2):
            if half == 0:
                store3(s3, 0, up[1], 2)
                fill3(s3, 2, sta, 0, 4)
                store3(a3, 0, up[0], 2)
                fill3(a3, 2, arr, 0, 4)
            else:
                fill3(s3, 6, sta, 12, 4)
                store3(s3, 10, down[1], 2)
                fill3(a3, 6, arr, 12, 4)
                store3(a3, 10, down[0], 2)
            pre = conv(s3, 6 * half, 4, w, 0, False)
            hid, slope = activate(pre)
            spot = lax.broadcasted_iota(jnp.int32, (4 * COLS, CH), 0) // COLS
            if half == 0:
                mask = jnp.where(spot == 0, has_up, 1.0)
            else:
                mask = jnp.where(spot == 3, has_down, 1.0)
            hid_e[rows(4 * half, 4), :] = (hid * mask).astype(BF16)
            slope_e[rows(4 * half, 4), :] = slope.astype(BF16)
            if leading:
                act, _ = activate(conv(a3, 6 * half, 4, w, 0, False))
            else:
                act = conv(a3, 6 * half, 4, w, 1, True) * slope
            act = act * mask
            act_e[rows(4 * half, 4), :] = act.astype(BF16)
            if half == 0:
                store3(c3, 0, act, 4)
                fill3(c3, 4, act_m, 0, 2)
            else:
                fill3(c3, 6, act_m, 8, 2)
                store3(c3, 8, act, 4)
            total = conv(c3, 6 * half, 4, w, 1 if leading else 0, not leading)
            kept = arr[rows(12 * half, 4), :].astype(F32)
            out_e[rows(4 * half, 4), :] = (total + kept).astype(BF16)

    by_role(body)


def kernel_c(
    got_m, arr, sta, up, down, act_m, act_e, hid_m, hid_e, slope_m, w, act2_m, grad, r3, y3, z3, whole
):
    def body(leading):
        fill3(r3, 0, got_m, 0, 8)
        total = conv(r3, 0, 6, w, 1 if leading else 0, leading)
        if leading:
            act = total * slope_m[rows(2, 6), :].astype(F32)
            act2_m[...] = act.astype(BF16)
            store3(z3, 0, act, 6)
            for a in range(3):
                put_grad(grad, 1, a, outer(hid_m[rows(a, 8), :], r3[rows(0, 8), :]))
                put_grad(grad, 0, a, outer(sta[rows(4 + a, 6), :], z3[rows(0, 6), :]))
        else:
            act, _ = activate(total)
            act2_m[...] = act.astype(BF16)

            def shift_arr(step):
                store3(y3, 2 * step, arr[rows(2 * step, 2), :], 2)

            repeat(8, shift_arr)
            whole[rows(0, 4), :] = hid_e[rows(0, 4), :]
            whole[rows(4, 10), :] = hid_m[...]
            whole[rows(14, 4), :] = hid_e[rows(4, 4), :]

            def second_grad(a):
                put_grad(grad, 1, a, outer(whole[rows(a, 16), :], y3[...]))

            def first_grad(a):
                put_grad(grad, 0, a, outer(whole[rows(a, 16), :], z3[...]))

            repeat(3, second_grad)
            fill3(z3, 0, act_e, 1, 3)
            fill3(z3, 3, act_m, 0, 10)
            fill3(z3, 13, act_e, 4, 3)
            whole[rows(0, 1), :] = up[1, rows(1, 1), :]
            whole[rows(1, 16), :] = sta[...]
            whole[rows(17, 1), :] = down[1, rows(0, 1), :]
            repeat(3, first_grad)

    by_role(body)


def kernel_d(got_m, got_e, sta, hid_m, hid_e, slope_m, slope_e, grad_in, w, act2_e, grad, r3, z3, h6):
    def body(leading):
        fill3(r3, 0, got_e, 0, 4)
        fill3(r3, 4, got_m, 0, 2)
        fill3(r3, 6, got_m, 6, 2)
        fill3(r3, 8, got_e, 4, 4)
        for half in range(2):
            total = conv(r3, 6 * half, 4, w, 1 if leading else 0, leading)
            if leading:
                if half == 0:
                    slope = jnp.concatenate([slope_e[rows(2, 2), :], slope_m[rows(0, 2), :]], axis=0)
                else:
                    slope = jnp.concatenate([slope_m[rows(8, 2), :], slope_e[rows(4, 2), :]], axis=0)
                act = total * slope.astype(F32)
                store3(z3, 4 * half, act, 4)
            else:
                act, _ = activate(total)
            act2_e[rows(4 * half, 4), :] = act.astype(BF16)
        if leading:
            h6[rows(0, 4), :] = hid_e[rows(0, 4), :]
            h6[rows(4, 2), :] = hid_m[rows(0, 2), :]
            h6[rows(6, 2), :] = hid_m[rows(8, 2), :]
            h6[rows(8, 4), :] = hid_e[rows(4, 4), :]
            for a in range(3):
                more = outer(h6[rows(a, 4), :], r3[rows(0, 4), :])
                more = more + outer(h6[rows(6 + a, 4), :], r3[rows(8, 4), :])
                put_grad(grad, 1, a, get_grad(grad_in, 1, a) + more)
                more = outer(sta[rows(a, 4), :], z3[rows(0, 4), :])
                more = more + outer(sta[rows(10 + a, 4), :], z3[rows(4, 4), :])
                put_grad(grad, 0, a, get_grad(grad_in, 0, a) + more)

    by_role(body)


def kernel_e(
    scale, got_e, got_up, got_down, sta, up, down, slope_e, grad_c, grad_d, w, act2_h, send, keep, r3, z3, x2, tot
):
    has_up, has_down = edge_flags()
    core = lax.axis_index("space_2")

    def emit(src, from_at, to_at, width):
        for pair in range(8):
            for dst, side in ((keep, core), (send, 1 - core)):
                first = pl.multiple_of(32 * pair + 8 * side, 8)
                second = pl.multiple_of(32 * pair + 16 + 8 * side, 8)
                val = jnp.concatenate(
                    [
                        src[pl.ds(first, 8), from_at : from_at + width],
                        src[pl.ds(second, 8), from_at : from_at + width],
                    ],
                    axis=0,
                )
                dst[pl.ds(16 * pair, 16), to_at : to_at + width] = (val * scale).astype(dst.dtype)

    def body(leading):
        store3(r3, 0, got_up[...], 2)
        fill3(r3, 2, got_e, 0, 2)
        fill3(r3, 4, got_e, 6, 2)
        store3(r3, 6, got_down[...], 2)
        spot = lax.broadcasted_iota(jnp.int32, (2 * COLS, CH), 0) // COLS
        for half in range(2):
            total = conv(r3, 4 * half, 2, w, 1 if leading else 0, leading)
            if leading:
                act = total * slope_e[rows(6 * half, 2), :].astype(F32)
            else:
                act, _ = activate(total)
            if half == 0:
                act = act * jnp.where(spot == 0, has_up, 1.0)
            else:
                act = act * jnp.where(spot == 1, has_down, 1.0)
            act2_h[rows(2 * half, 2), :] = act.astype(BF16)
        if leading:
            store3(z3, 0, act2_h[rows(1, 2), :], 2)
            x2[rows(0, 1), :] = up[1, rows(1, 1), :]
            x2[rows(1, 2), :] = sta[rows(0, 2), :]
            x2[rows(3, 2), :] = sta[rows(14, 2), :]
            x2[rows(5, 1), :] = down[1, rows(0, 1), :]
            for a in range(3):
                left = jnp.concatenate([x2[rows(a, 1), :], x2[rows(3 + a, 1), :]], axis=0)
                put_grad(tot, 0, a, get_grad(grad_d, 0, a) + outer(left, z3[...]))
            emit(tot, 0, 0, TAPS)
            emit(grad_d, TAPS, TAPS, TAPS)
        else:
            emit(grad_c, 0, 0, 2 * TAPS)

    by_role(body)


def kernel_f(got_m, got_e, act2_m, act2_e, act2_h, w, out, c3, kept):
    def body(leading):
        fill3(c3, 0, act2_h, 0, 2)
        fill3(c3, 2, act2_e, 0, 4)
        fill3(c3, 6, act2_m, 0, 6)
        fill3(c3, 12, act2_e, 4, 4)
        fill3(c3, 16, act2_h, 2, 2)
        kept[rows(0, 4), :] = got_e[rows(0, 4), :]
        kept[rows(4, 8), :] = got_m[...]
        kept[rows(12, 4), :] = got_e[rows(4, 4), :]

        def block(step):
            row = 4 * step
            total = conv(c3, row, 4, w, 0 if leading else 1, leading)
            out[rows(row, 4), :] = (total + kept[rows(row, 4), :].astype(F32)).astype(BF16)

        repeat(4, block)

    by_role(body)


def call(body, outs, scratch, args, row_units, limit=18, space=pltpu.VMEM, sems=0):
    block = pl.BlockSpec(memory_space=pltpu.VMEM)
    semaphores = [pltpu.SemaphoreType.DMA((sems,))] if sems else []
    return pl.pallas_call(
        body,
        out_shape=[jax.ShapeDtypeStruct(shape, dtype) for shape, dtype in outs],
        in_specs=[pl.BlockSpec(memory_space=space)] * len(args),
        out_specs=[block] * len(outs),
        scratch_shapes=[pltpu.VMEM(shape, dtype) for shape, dtype in scratch] + semaphores,
        compiler_params=pltpu.CompilerParams(vmem_limit_bytes=limit * MIB),
        cost_estimate=pl.CostEstimate(
            flops=int(row_units * 2 * COLS * TAPS * CH),
            bytes_accessed=4 * MIB,
            transcendentals=0,
        ),
    )(*args)


def tick(arrivals, stashed, weights):
    arr = arrivals.reshape(-1, CH)
    sta = stashed.reshape(-1, CH)
    w = weights[0, 0]
    tile = arr.shape[0] // COLS
    space = lax.axis_size(SPACE)
    scale = 1.0 / math.sqrt(tile * space * COLS)

    def img(count, dtype=BF16):
        return ((count * COLS, CH), dtype)

    def img3(count):
        return ((count * COLS, 3 * CH), BF16)

    grad_shape = ((CH, 2 * TAPS), F32)

    two = 2 * COLS
    edge = ((2, two, CH), BF16)
    out_m, act_m, hid_m, slope_m, low, high, sta_v = call(
        kernel_a,
        [img(8), img(10), img(10), img(10), edge, edge, img(16)],
        [img3(12), img3(12), img3(10), (w.shape, BF16), img(16), img(10, F32)],
        (arr, sta, w),
        28,
        limit=LIMIT_A,
        space=pltpu.HBM,
        sems=8,
    )
    sta = sta_v
    ahead = [(i, i + 1) for i in range(space - 1)]
    back = [(j, i) for i, j in ahead]
    swap = [(0, 1), (1, 0)]
    got_m = lax.ppermute(out_m, "segment", swap)
    up = lax.ppermute(low, SPACE, ahead)
    down = lax.ppermute(high, SPACE, back)
    out_e, act_e, hid_e, slope_e = call(
        kernel_b,
        [img(8), img(8), img(8), img(8)],
        [img3(12), img3(12), img3(12)],
        (arr, sta, up, down, act_m, w),
        24,
    )
    got_e = lax.ppermute(out_e, "segment", swap)
    both = ("segment",) + SPACE
    across_ahead = [((s * space + i), ((1 - s) * space + j)) for s in range(2) for i, j in ahead]
    across_back = [((s * space + i), ((1 - s) * space + j)) for s in range(2) for i, j in back]
    got_up = lax.ppermute(out_e[-two:], both, across_ahead)
    got_down = lax.ppermute(out_e[:two], both, across_back)
    act2_m, grad_c = call(
        kernel_c,
        [img(6), grad_shape],
        [img3(8), img3(16), img3(16), img(18)],
        (got_m, arr, sta, up, down, act_m, act_e, hid_m, hid_e, slope_m, w),
        38,
    )
    act2_e, grad_d = call(
        kernel_d,
        [img(8), grad_shape],
        [img3(12), img3(8), img(12)],
        (got_m, got_e, sta, hid_m, hid_e, slope_m, slope_e, grad_c, w),
        24,
    )
    act2_h, sent, keep = call(
        functools.partial(kernel_e, scale),
        [img(4), ((CH // 2, 2 * TAPS), BF16), ((CH // 2, 2 * TAPS), F32)],
        [img3(8), img3(2), img(6), ((CH, TAPS), F32)],
        (got_e, got_up, got_down, sta, up, down, slope_e, grad_c, grad_d, w),
        8,
    )
    (departing,) = call(
        kernel_f, [img(16)], [img3(18), img(16)], (got_m, got_e, act2_m, act2_e, act2_h, w), 16
    )

    chips = space // 2
    share = CH // space
    other = lax.ppermute(sent, "space_2", swap)
    pieces = (keep + other.astype(F32)).astype(BF16).reshape(chips, share, 2 * TAPS)
    pieces = lax.all_to_all(pieces, ("space_0", "space_1"), 0, 0, tiled=True)
    owned = jnp.sum(pieces.astype(F32), axis=0)
    owned, departing = lax.optimization_barrier((owned, departing))
    pairs = [(i, i ^ 3) for i in range(4)]
    partner = lax.ppermute(owned.astype(BF16), ("segment", "mirror"), pairs)
    combined = owned + partner.astype(F32)
    return (
        departing.reshape(arrivals.shape),
        combined.reshape(1, 1, share, 2, 3, 3, CH),
    )


def solution(mesh):
    split = Mesh(
        mesh.devices.reshape(mesh.shape["segment"], 4, 4, 2, mesh.shape["mirror"]),
        ("segment", "space_0", "space_1", "space_2", "mirror"),
    )
    in_specs = (
        P("mirror", "segment", SPACE, None, None),
        P("mirror", "segment", SPACE, None, None),
        P("mirror", "segment", None, None, None, None, None),
    )
    out_specs = (
        P("mirror", "segment", SPACE, None, None),
        P("mirror", "segment", SPACE, None, None, None, None),
    )
    return jax.shard_map(tick, mesh=split, in_specs=in_specs, out_specs=out_specs, check_vma=False)
```

```python
import functools
import math

import jax
import jax.numpy as jnp
from jax import lax
from jax.experimental import pallas as pl
from jax.experimental.pallas import tpu as pltpu
from jax.sharding import Mesh
from jax.sharding import PartitionSpec as P

SPACE = ("space_0", "space_1", "space_2")
BF16 = jnp.bfloat16
F32 = jnp.float32
COLS = 128
CH = 256
TAPS = 9 * CH
MIB = 1 << 20
LIMIT_A = 50


def rows(first, count):
    start = first * COLS
    if not isinstance(start, int):
        start = pl.multiple_of(start, COLS)
    return pl.ds(start, count * COLS)


def repeat(steps, body):
    def step(index, carry):
        body(index)
        return carry

    lax.fori_loop(0, steps, step, 0)


def store3(dst, row, val, count):
    size = count * COLS
    col = lax.broadcasted_iota(jnp.int32, (size, CH), 0) & (COLS - 1)
    val = val.astype(F32)
    left = jnp.where(col == 0, 0.0, pltpu.roll(val, 1, 0))
    right = jnp.where(col == COLS - 1, 0.0, pltpu.roll(val, size - 1, 0))
    where = rows(row, count)
    dst[where, 0:CH] = left.astype(BF16)
    dst[where, CH : 2 * CH] = val.astype(BF16)
    dst[where, 2 * CH :] = right.astype(BF16)


def fill3(dst, row, src, first, count):
    for step in range(0, count, 2):
        size = min(2, count - step)
        store3(dst, row + step, src[rows(first + step, size), :], size)


def conv(src3, first, count, weights, which, transposed):
    total = None
    for a in range(3):
        for b in range(3):
            window = src3[rows(first + a, count), b * CH : (b + 1) * CH]
            if transposed:
                part = lax.dot_general(
                    window,
                    weights[which, 2 - a, 2 - b],
                    (((1,), (1,)), ((), ())),
                    preferred_element_type=F32,
                )
            else:
                part = jnp.dot(window, weights[which, a, b], preferred_element_type=F32)
            total = part if total is None else total + part
    return total


def outer(left, right):
    return lax.dot_general(left, right, (((0,), (0,)), ((), ())), preferred_element_type=F32)


def put_grad(dst, conv_index, a, val):
    for b in range(3):
        at = conv_index * TAPS + (3 * a + b) * CH
        if not isinstance(at, int):
            at = pl.multiple_of(at, CH)
        dst[:, pl.ds(at, CH)] = val[:, (2 - b) * CH : (3 - b) * CH]


def get_grad(src, conv_index, a):
    parts = []
    for b in (2, 1, 0):
        at = conv_index * TAPS + (3 * a + b) * CH
        parts.append(src[:, at : at + CH])
    return jnp.concatenate(parts, axis=1)


def activate(pre):
    sig = jax.nn.sigmoid(pre)
    return pre * sig, sig * (1.0 + pre * (1.0 - sig))


def is_leading():
    return lax.axis_index("segment") == lax.axis_index("mirror")


def by_role(body):
    leading = is_leading()

    @pl.when(leading)
    def _():
        body(True)

    @pl.when(jnp.logical_not(leading))
    def _():
        body(False)


def edge_flags():
    place = lax.axis_index(SPACE)
    count = lax.axis_size(SPACE)
    return (place > 0).astype(F32), (place < count - 1).astype(F32)


def above(near, far):
    return jnp.where(lax.axis_index("space_2") == 1, near.astype(F32), far.astype(F32))


def below(near, far):
    return jnp.where(lax.axis_index("space_2") == 0, near.astype(F32), far.astype(F32))


def kernel_a(
    arr_hbm, sta_hbm, w_hbm, out_m, act_m, hid_m, slope_m, near, far, sta, s3, a3, c3, w, arr, steep, sems
):
    two = 2 * COLS
    size = arr_hbm.shape[0]
    core = lax.axis_index("space_2")
    inner_at = pl.ds(pl.multiple_of((1 - core) * (size - two), two), two)
    outer_at = pl.ds(pl.multiple_of(core * (size - two), two), two)
    moves = (
        (sta_hbm, sta),
        (w_hbm.at[0], w.at[0]),
        (arr_hbm, arr),
        (w_hbm.at[1], w.at[1]),
        (arr_hbm.at[inner_at], near.at[0]),
        (sta_hbm.at[inner_at], near.at[1]),
        (arr_hbm.at[outer_at], far.at[0]),
        (sta_hbm.at[outer_at], far.at[1]),
    )
    copies = [pltpu.make_async_copy(src, dst, sems.at[i]) for i, (src, dst) in enumerate(moves)]
    for copy in copies:
        copy.start()
    for copy in copies[:3]:
        copy.wait()

    def body(leading):
        fill3(s3, 0, sta, 2, 12)
        fill3(a3, 0, arr, 2, 12)
        for row in (0, 5):
            pre = conv(s3, row, 5, w, 0, False)
            hid, slope = activate(pre)
            hid_m[rows(row, 5), :] = hid.astype(BF16)
            if leading:
                slope_m[rows(row, 5), :] = slope.astype(BF16)
            else:
                steep[rows(row, 5), :] = slope
        for copy in copies[3:]:
            copy.wait()
        for row in (0, 5):
            if leading:
                act, _ = activate(conv(a3, row, 5, w, 0, False))
            else:
                act = conv(a3, row, 5, w, 1, True) * steep[rows(row, 5), :]
            act_m[rows(row, 5), :] = act.astype(BF16)
            store3(c3, row, act, 5)
        for row in (0, 4):
            total = conv(c3, row, 4, w, 1 if leading else 0, not leading)
            out_m[rows(row, 4), :] = (total + arr[rows(4 + row, 4), :].astype(F32)).astype(BF16)

    by_role(body)


def kernel_b(arr, sta, near, far, act_m, w, out_e, act_e, hid_e, slope_e, border, s3, a3, c3):
    has_up, has_down = edge_flags()

    def body(leading):
        for half in range(2):
            if half == 0:
                up = above(near[1], far[1])
                border[rows(0, 1), :] = up[COLS:].astype(BF16)
                store3(s3, 0, up, 2)
                fill3(s3, 2, sta, 0, 4)
                store3(a3, 0, above(near[0], far[0]), 2)
                fill3(a3, 2, arr, 0, 4)
            else:
                fill3(s3, 6, sta, 12, 4)
                down = below(near[1], far[1])
                border[rows(1, 1), :] = down[:COLS].astype(BF16)
                store3(s3, 10, down, 2)
                fill3(a3, 6, arr, 12, 4)
                store3(a3, 10, below(near[0], far[0]), 2)
            pre = conv(s3, 6 * half, 4, w, 0, False)
            hid, slope = activate(pre)
            spot = lax.broadcasted_iota(jnp.int32, (4 * COLS, CH), 0) // COLS
            if half == 0:
                mask = jnp.where(spot == 0, has_up, 1.0)
            else:
                mask = jnp.where(spot == 3, has_down, 1.0)
            hid_e[rows(4 * half, 4), :] = (hid * mask).astype(BF16)
            slope_e[rows(4 * half, 4), :] = slope.astype(BF16)
            if leading:
                act, _ = activate(conv(a3, 6 * half, 4, w, 0, False))
            else:
                act = conv(a3, 6 * half, 4, w, 1, True) * slope
            act = act * mask
            act_e[rows(4 * half, 4), :] = act.astype(BF16)
            if half == 0:
                store3(c3, 0, act, 4)
                fill3(c3, 4, act_m, 0, 2)
            else:
                fill3(c3, 6, act_m, 8, 2)
                store3(c3, 8, act, 4)
            total = conv(c3, 6 * half, 4, w, 1 if leading else 0, not leading)
            kept = arr[rows(12 * half, 4), :].astype(F32)
            out_e[rows(4 * half, 4), :] = (total + kept).astype(BF16)

    by_role(body)


def kernel_c(
    got_m, arr, sta, border, act_m, act_e, hid_m, hid_e, slope_m, w, act2_m, grad, r3, y3, z3, whole
):
    def body(leading):
        fill3(r3, 0, got_m, 0, 8)
        total = conv(r3, 0, 6, w, 1 if leading else 0, leading)
        if leading:
            act = total * slope_m[rows(2, 6), :].astype(F32)
            act2_m[...] = act.astype(BF16)
            store3(z3, 0, act, 6)
            for a in range(3):
                put_grad(grad, 1, a, outer(hid_m[rows(a, 8), :], r3[rows(0, 8), :]))
                put_grad(grad, 0, a, outer(sta[rows(4 + a, 6), :], z3[rows(0, 6), :]))
        else:
            act, _ = activate(total)
            act2_m[...] = act.astype(BF16)

            def shift_arr(step):
                store3(y3, 2 * step, arr[rows(2 * step, 2), :], 2)

            repeat(8, shift_arr)
            whole[rows(0, 4), :] = hid_e[rows(0, 4), :]
            whole[rows(4, 10), :] = hid_m[...]
            whole[rows(14, 4), :] = hid_e[rows(4, 4), :]

            def second_grad(a):
                put_grad(grad, 1, a, outer(whole[rows(a, 16), :], y3[...]))

            def first_grad(a):
                put_grad(grad, 0, a, outer(whole[rows(a, 16), :], z3[...]))

            repeat(3, second_grad)
            fill3(z3, 0, act_e, 1, 3)
            fill3(z3, 3, act_m, 0, 10)
            fill3(z3, 13, act_e, 4, 3)
            whole[rows(0, 1), :] = border[rows(0, 1), :]
            whole[rows(1, 16), :] = sta[...]
            whole[rows(17, 1), :] = border[rows(1, 1), :]
            repeat(3, first_grad)

    by_role(body)


def kernel_d(got_m, got_e, sta, hid_m, hid_e, slope_m, slope_e, grad_in, w, act2_e, grad, r3, z3, h6):
    def body(leading):
        fill3(r3, 0, got_e, 0, 4)
        fill3(r3, 4, got_m, 0, 2)
        fill3(r3, 6, got_m, 6, 2)
        fill3(r3, 8, got_e, 4, 4)
        for half in range(2):
            total = conv(r3, 6 * half, 4, w, 1 if leading else 0, leading)
            if leading:
                if half == 0:
                    slope = jnp.concatenate([slope_e[rows(2, 2), :], slope_m[rows(0, 2), :]], axis=0)
                else:
                    slope = jnp.concatenate([slope_m[rows(8, 2), :], slope_e[rows(4, 2), :]], axis=0)
                act = total * slope.astype(F32)
                store3(z3, 4 * half, act, 4)
            else:
                act, _ = activate(total)
            act2_e[rows(4 * half, 4), :] = act.astype(BF16)
        if leading:
            h6[rows(0, 4), :] = hid_e[rows(0, 4), :]
            h6[rows(4, 2), :] = hid_m[rows(0, 2), :]
            h6[rows(6, 2), :] = hid_m[rows(8, 2), :]
            h6[rows(8, 4), :] = hid_e[rows(4, 4), :]
            for a in range(3):
                more = outer(h6[rows(a, 4), :], r3[rows(0, 4), :])
                more = more + outer(h6[rows(6 + a, 4), :], r3[rows(8, 4), :])
                put_grad(grad, 1, a, get_grad(grad_in, 1, a) + more)
                more = outer(sta[rows(a, 4), :], z3[rows(0, 4), :])
                more = more + outer(sta[rows(10 + a, 4), :], z3[rows(4, 4), :])
                put_grad(grad, 0, a, get_grad(grad_in, 0, a) + more)

    by_role(body)


def kernel_e(
    scale, got_e, got_near, got_far, sta, border, slope_e, grad_c, grad_d, w, act2_h, send, keep, r3, z3, x2, tot
):
    has_up, has_down = edge_flags()
    core = lax.axis_index("space_2")

    def emit(src, from_at, to_at, width):
        for pair in range(8):
            for dst, side in ((keep, core), (send, 1 - core)):
                first = pl.multiple_of(32 * pair + 8 * side, 8)
                second = pl.multiple_of(32 * pair + 16 + 8 * side, 8)
                val = jnp.concatenate(
                    [
                        src[pl.ds(first, 8), from_at : from_at + width],
                        src[pl.ds(second, 8), from_at : from_at + width],
                    ],
                    axis=0,
                )
                dst[pl.ds(16 * pair, 16), to_at : to_at + width] = (val * scale).astype(dst.dtype)

    def body(leading):
        store3(r3, 0, above(got_near[...], got_far[...]), 2)
        fill3(r3, 2, got_e, 0, 2)
        fill3(r3, 4, got_e, 6, 2)
        store3(r3, 6, below(got_near[...], got_far[...]), 2)
        spot = lax.broadcasted_iota(jnp.int32, (2 * COLS, CH), 0) // COLS
        for half in range(2):
            total = conv(r3, 4 * half, 2, w, 1 if leading else 0, leading)
            if leading:
                act = total * slope_e[rows(6 * half, 2), :].astype(F32)
            else:
                act, _ = activate(total)
            if half == 0:
                act = act * jnp.where(spot == 0, has_up, 1.0)
            else:
                act = act * jnp.where(spot == 1, has_down, 1.0)
            act2_h[rows(2 * half, 2), :] = act.astype(BF16)
        if leading:
            store3(z3, 0, act2_h[rows(1, 2), :], 2)
            x2[rows(0, 1), :] = border[rows(0, 1), :]
            x2[rows(1, 2), :] = sta[rows(0, 2), :]
            x2[rows(3, 2), :] = sta[rows(14, 2), :]
            x2[rows(5, 1), :] = border[rows(1, 1), :]
            for a in range(3):
                left = jnp.concatenate([x2[rows(a, 1), :], x2[rows(3 + a, 1), :]], axis=0)
                put_grad(tot, 0, a, get_grad(grad_d, 0, a) + outer(left, z3[...]))
            emit(tot, 0, 0, TAPS)
            emit(grad_d, TAPS, TAPS, TAPS)
        else:
            emit(grad_c, 0, 0, 2 * TAPS)

    by_role(body)


def kernel_pick(got_e, inner, outer):
    core = lax.axis_index("space_2")
    inner[...] = got_e[rows(6 * (1 - core), 2), :]
    outer[...] = got_e[rows(6 * core, 2), :]


def kernel_sum(keep, other, total):
    for row in range(0, keep.shape[0], 16):
        part = pl.ds(row, 16)
        total[part, :] = (keep[part, :] + other[part, :].astype(F32)).astype(BF16)


def kernel_f(got_m, got_e, act2_m, act2_e, act2_h, w, out, c3, kept):
    def body(leading):
        fill3(c3, 0, act2_h, 0, 2)
        fill3(c3, 2, act2_e, 0, 4)
        fill3(c3, 6, act2_m, 0, 6)
        fill3(c3, 12, act2_e, 4, 4)
        fill3(c3, 16, act2_h, 2, 2)
        kept[rows(0, 4), :] = got_e[rows(0, 4), :]
        kept[rows(4, 8), :] = got_m[...]
        kept[rows(12, 4), :] = got_e[rows(4, 4), :]

        def block(step):
            row = 4 * step
            total = conv(c3, row, 4, w, 0 if leading else 1, leading)
            out[rows(row, 4), :] = (total + kept[rows(row, 4), :].astype(F32)).astype(BF16)

        repeat(4, block)

    by_role(body)


def call(body, outs, scratch, args, row_units, limit=18, space=pltpu.VMEM, sems=0):
    block = pl.BlockSpec(memory_space=pltpu.VMEM)
    semaphores = [pltpu.SemaphoreType.DMA((sems,))] if sems else []
    return pl.pallas_call(
        body,
        out_shape=[jax.ShapeDtypeStruct(shape, dtype) for shape, dtype in outs],
        in_specs=[pl.BlockSpec(memory_space=space)] * len(args),
        out_specs=[block] * len(outs),
        scratch_shapes=[pltpu.VMEM(shape, dtype) for shape, dtype in scratch] + semaphores,
        compiler_params=pltpu.CompilerParams(vmem_limit_bytes=limit * MIB),
        cost_estimate=pl.CostEstimate(
            flops=int(row_units * 2 * COLS * TAPS * CH),
            bytes_accessed=4 * MIB,
            transcendentals=0,
        ),
    )(*args)


def tick(arrivals, stashed, weights):
    arr = arrivals.reshape(-1, CH)
    sta = stashed.reshape(-1, CH)
    w = weights[0, 0]
    tile = arr.shape[0] // COLS
    space = lax.axis_size(SPACE)
    scale = 1.0 / math.sqrt(tile * space * COLS)

    def img(count, dtype=BF16):
        return ((count * COLS, CH), dtype)

    def img3(count):
        return ((count * COLS, 3 * CH), BF16)

    grad_shape = ((CH, 2 * TAPS), F32)

    two = 2 * COLS
    edge = ((2, two, CH), BF16)
    out_m, act_m, hid_m, slope_m, near, far, sta_v = call(
        kernel_a,
        [img(8), img(10), img(10), img(10), edge, edge, img(16)],
        [img3(12), img3(12), img3(10), (w.shape, BF16), img(16), img(10, F32)],
        (arr, sta, w),
        28,
        limit=LIMIT_A,
        space=pltpu.HBM,
        sems=8,
    )
    sta = sta_v
    hop = [(i, i + 1) for i in range(1, space - 1, 2)]
    hop = hop + [(j, i) for i, j in hop]
    swap = [(0, 1), (1, 0)]
    got_m = lax.ppermute(out_m, "segment", swap)
    near = lax.ppermute(near, "space_2", swap)
    far = lax.ppermute(far, SPACE, hop)
    out_e, act_e, hid_e, slope_e, border = call(
        kernel_b,
        [img(8), img(8), img(8), img(8), img(2)],
        [img3(12), img3(12), img3(12)],
        (arr, sta, near, far, act_m, w),
        24,
    )
    got_e = lax.ppermute(out_e, "segment", swap)
    inner_rows, outer_rows = call(kernel_pick, [img(2), img(2)], [], (got_e,), 0, limit=4)
    got_near = lax.ppermute(inner_rows, "space_2", swap)
    got_far = lax.ppermute(outer_rows, SPACE, hop)
    act2_m, grad_c = call(
        kernel_c,
        [img(6), grad_shape],
        [img3(8), img3(16), img3(16), img(18)],
        (got_m, arr, sta, border, act_m, act_e, hid_m, hid_e, slope_m, w),
        38,
    )
    act2_e, grad_d = call(
        kernel_d,
        [img(8), grad_shape],
        [img3(12), img3(8), img(12)],
        (got_m, got_e, sta, hid_m, hid_e, slope_m, slope_e, grad_c, w),
        24,
    )
    act2_h, sent, keep = call(
        functools.partial(kernel_e, scale),
        [img(4), ((CH // 2, 2 * TAPS), BF16), ((CH // 2, 2 * TAPS), F32)],
        [img3(8), img3(2), img(6), ((CH, TAPS), F32)],
        (got_e, got_near, got_far, sta, border, slope_e, grad_c, grad_d, w),
        8,
    )
    (departing,) = call(
        kernel_f, [img(16)], [img3(18), img(16)], (got_m, got_e, act2_m, act2_e, act2_h, w), 16
    )

    chips = space // 2
    share = CH // space
    other = lax.ppermute(sent, "space_2", swap)
    (pieces,) = call(kernel_sum, [(keep.shape, BF16)], [], (keep, other), 0, limit=8)
    pieces = pieces.reshape(chips, share, 2 * TAPS)
    pieces = lax.all_to_all(pieces, ("space_0", "space_1"), 0, 0, tiled=True)
    owned = jnp.sum(pieces.astype(F32), axis=0)
    owned, departing = lax.optimization_barrier((owned, departing))
    pairs = [(i, i ^ 3) for i in range(4)]
    partner = lax.ppermute(owned.astype(BF16), ("segment", "mirror"), pairs)
    combined = owned + partner.astype(F32)
    return (
        departing.reshape(arrivals.shape),
        combined.reshape(1, 1, share, 2, 3, 3, CH),
    )


def solution(mesh):
    split = Mesh(
        mesh.devices.reshape(mesh.shape["segment"], 4, 4, 2, mesh.shape["mirror"]),
        ("segment", "space_0", "space_1", "space_2", "mirror"),
    )
    in_specs = (
        P("mirror", "segment", SPACE, None, None),
        P("mirror", "segment", SPACE, None, None),
        P("mirror", "segment", None, None, None, None, None),
    )
    out_specs = (
        P("mirror", "segment", SPACE, None, None),
        P("mirror", "segment", SPACE, None, None, None, None),
    )
    return jax.shard_map(tick, mesh=split, in_specs=in_specs, out_specs=out_specs, check_vma=False)
```

```python
import functools
import math

import jax
import jax.numpy as jnp
from jax import lax
from jax.experimental import pallas as pl
from jax.experimental.pallas import tpu as pltpu
from jax.sharding import Mesh
from jax.sharding import PartitionSpec as P

SPACE = ("space_0", "space_1", "space_2")
BF16 = jnp.bfloat16
F32 = jnp.float32
COLS = 128
CH = 256
TAPS = 9 * CH
MIB = 1 << 20
LIMIT_A = 50


def rows(first, count):
    start = first * COLS
    if not isinstance(start, int):
        start = pl.multiple_of(start, COLS)
    return pl.ds(start, count * COLS)


def repeat(steps, body):
    def step(index, carry):
        body(index)
        return carry

    lax.fori_loop(0, steps, step, 0)


def store3(dst, row, val, count):
    size = count * COLS
    col = lax.broadcasted_iota(jnp.int32, (size, CH), 0) & (COLS - 1)
    val = val.astype(F32)
    left = jnp.where(col == 0, 0.0, pltpu.roll(val, 1, 0))
    right = jnp.where(col == COLS - 1, 0.0, pltpu.roll(val, size - 1, 0))
    where = rows(row, count)
    dst[where, 0:CH] = left.astype(BF16)
    dst[where, CH : 2 * CH] = val.astype(BF16)
    dst[where, 2 * CH :] = right.astype(BF16)


def fill3(dst, row, src, first, count):
    for step in range(0, count, 2):
        size = min(2, count - step)
        store3(dst, row + step, src[rows(first + step, size), :], size)


def conv(src3, first, count, weights, which, transposed):
    firsts = first if isinstance(first, tuple) else (first,)
    total = None
    for a in range(3):
        for b in range(3):
            parts = [src3[rows(at + a, count), b * CH : (b + 1) * CH] for at in firsts]
            window = parts[0] if len(parts) == 1 else jnp.concatenate(parts, axis=0)
            if transposed:
                part = lax.dot_general(
                    window,
                    weights[which, 2 - a, 2 - b],
                    (((1,), (1,)), ((), ())),
                    preferred_element_type=F32,
                )
            else:
                part = jnp.dot(window, weights[which, a, b], preferred_element_type=F32)
            total = part if total is None else total + part
    return total


def outer(left, right):
    return lax.dot_general(left, right, (((0,), (0,)), ((), ())), preferred_element_type=F32)


def put_grad(dst, conv_index, a, val):
    for b in range(3):
        at = conv_index * TAPS + (3 * a + b) * CH
        if not isinstance(at, int):
            at = pl.multiple_of(at, CH)
        dst[:, pl.ds(at, CH)] = val[:, (2 - b) * CH : (3 - b) * CH]


def get_grad(src, conv_index, a):
    parts = []
    for b in (2, 1, 0):
        at = conv_index * TAPS + (3 * a + b) * CH
        parts.append(src[:, at : at + CH])
    return jnp.concatenate(parts, axis=1)


def activate(pre):
    sig = jax.nn.sigmoid(pre)
    return pre * sig, sig * (1.0 + pre * (1.0 - sig))


def is_leading():
    return lax.axis_index("segment") == lax.axis_index("mirror")


def by_role(body):
    leading = is_leading()

    @pl.when(leading)
    def _():
        body(True)

    @pl.when(jnp.logical_not(leading))
    def _():
        body(False)


def edge_flags():
    place = lax.axis_index(SPACE)
    count = lax.axis_size(SPACE)
    return (place > 0).astype(F32), (place < count - 1).astype(F32)


def above(near, far):
    return jnp.where(lax.axis_index("space_2") == 1, near.astype(F32), far.astype(F32))


def below(near, far):
    return jnp.where(lax.axis_index("space_2") == 0, near.astype(F32), far.astype(F32))


def kernel_a(
    arr_hbm, sta_hbm, w_hbm, out_m, act_m, hid_m, slope_m, near, far, sta, s3, a3, c3, w, arr, steep, sems
):
    two = 2 * COLS
    size = arr_hbm.shape[0]
    core = lax.axis_index("space_2")
    inner_at = pl.ds(pl.multiple_of((1 - core) * (size - two), two), two)
    outer_at = pl.ds(pl.multiple_of(core * (size - two), two), two)
    moves = (
        (sta_hbm, sta),
        (w_hbm.at[0], w.at[0]),
        (arr_hbm, arr),
        (w_hbm.at[1], w.at[1]),
        (arr_hbm.at[inner_at], near.at[0]),
        (sta_hbm.at[inner_at], near.at[1]),
        (arr_hbm.at[outer_at], far.at[0]),
        (sta_hbm.at[outer_at], far.at[1]),
    )
    copies = [pltpu.make_async_copy(src, dst, sems.at[i]) for i, (src, dst) in enumerate(moves)]
    for copy in copies:
        copy.start()
    for copy in copies[:2]:
        copy.wait()
    fill3(s3, 0, sta, 2, 12)
    for row in (0, 5):
        hid, slope = activate(conv(s3, row, 5, w, 0, False))
        hid_m[rows(row, 5), :] = hid.astype(BF16)
        slope_m[rows(row, 5), :] = slope.astype(BF16)
        steep[rows(row, 5), :] = slope
    for copy in copies[2:]:
        copy.wait()

    def body(leading):
        fill3(a3, 0, arr, 2, 12)
        for row in (0, 5):
            if leading:
                act, _ = activate(conv(a3, row, 5, w, 0, False))
            else:
                act = conv(a3, row, 5, w, 1, True) * steep[rows(row, 5), :]
            act_m[rows(row, 5), :] = act.astype(BF16)
            store3(c3, row, act, 5)
        for row in (0, 4):
            total = conv(c3, row, 4, w, 1 if leading else 0, not leading)
            out_m[rows(row, 4), :] = (total + arr[rows(4 + row, 4), :].astype(F32)).astype(BF16)

    by_role(body)


def kernel_q(arr, sta, act_m, w, out_q, act_q, hid_q, slope_q, s3, a3, c3, steep):
    fill3(s3, 0, sta, 0, 4)
    fill3(s3, 4, sta, 12, 4)
    hid, slope = activate(conv(s3, (0, 4), 2, w, 0, False))
    hid_q[...] = hid.astype(BF16)
    slope_q[...] = slope.astype(BF16)
    steep[...] = slope

    def body(leading):
        fill3(a3, 0, arr, 0, 4)
        fill3(a3, 4, arr, 12, 4)
        fill3(c3, 2, act_m, 0, 2)
        fill3(c3, 4, act_m, 8, 2)
        if leading:
            act, _ = activate(conv(a3, (0, 4), 2, w, 0, False))
        else:
            act = conv(a3, (0, 4), 2, w, 1, True) * steep[...]
        act_q[...] = act.astype(BF16)
        store3(c3, 0, act[: 2 * COLS], 2)
        store3(c3, 6, act[2 * COLS :], 2)
        total = conv(c3, (0, 4), 2, w, 1 if leading else 0, not leading)
        for half in range(2):
            kept = arr[rows(2 + 10 * half, 2), :].astype(F32)
            out_q[rows(2 * half, 2), :] = (total[2 * half * COLS : (2 * half + 2) * COLS] + kept).astype(BF16)

    by_role(body)


def kernel_b(
    arr, sta, near, far, out_q, act_q, hid_q, slope_q, w, out_e, act_e, hid_e, slope_e, border, s3, a3, c3, steep
):
    has_up, has_down = edge_flags()

    def spread(dst, mid, val):
        val = val.astype(BF16)
        dst[rows(0, 2), :] = val[: 2 * COLS]
        dst[rows(2, 4), :] = mid[...]
        dst[rows(6, 2), :] = val[2 * COLS :]

    up, down = above(near[1], far[1]), below(near[1], far[1])
    border[rows(0, 1), :] = up[COLS:].astype(BF16)
    border[rows(1, 1), :] = down[:COLS].astype(BF16)
    store3(s3, 0, up, 2)
    fill3(s3, 2, sta, 0, 2)
    fill3(s3, 4, sta, 14, 2)
    store3(s3, 6, down, 2)
    spot = lax.broadcasted_iota(jnp.int32, (4 * COLS, CH), 0) // COLS
    mask = jnp.where(spot == 0, has_up, jnp.where(spot == 3, has_down, 1.0))
    hid, slope = activate(conv(s3, (0, 4), 2, w, 0, False))
    spread(hid_e, hid_q, hid * mask)
    spread(slope_e, slope_q, slope)
    steep[...] = slope * mask

    def body(leading):
        store3(a3, 0, above(near[0], far[0]), 2)
        fill3(a3, 2, arr, 0, 2)
        fill3(a3, 4, arr, 14, 2)
        store3(a3, 6, below(near[0], far[0]), 2)
        fill3(c3, 2, act_q, 0, 2)
        fill3(c3, 4, act_q, 2, 2)
        if leading:
            act, _ = activate(conv(a3, (0, 4), 2, w, 0, False))
            spot = lax.broadcasted_iota(jnp.int32, (4 * COLS, CH), 0) // COLS
            act = act * jnp.where(spot == 0, has_up, jnp.where(spot == 3, has_down, 1.0))
        else:
            act = conv(a3, (0, 4), 2, w, 1, True) * steep[...]
        spread(act_e, act_q, act)
        store3(c3, 0, act[: 2 * COLS], 2)
        store3(c3, 6, act[2 * COLS :], 2)
        total = conv(c3, (0, 4), 2, w, 1 if leading else 0, not leading)
        for half in range(2):
            kept = arr[rows(14 * half, 2), :].astype(F32)
            part = total[2 * half * COLS : (2 * half + 2) * COLS] + kept
            out_e[rows(6 * half, 2), :] = part.astype(BF16)
        out_e[rows(2, 4), :] = out_q[...]

    by_role(body)


def kernel_c(
    got_m, arr, sta, border, act_m, act_e, hid_m, hid_e, slope_m, w, act2_m, grad, r3, y3, z3, whole
):
    def body(leading):
        fill3(r3, 0, got_m, 0, 8)
        total = conv(r3, 0, 6, w, 1 if leading else 0, leading)
        if leading:
            act = total * slope_m[rows(2, 6), :].astype(F32)
            act2_m[...] = act.astype(BF16)
            store3(z3, 0, act, 6)
            for a in range(3):
                put_grad(grad, 1, a, outer(hid_m[rows(a, 8), :], r3[rows(0, 8), :]))
                put_grad(grad, 0, a, outer(sta[rows(4 + a, 6), :], z3[rows(0, 6), :]))
        else:
            act, _ = activate(total)
            act2_m[...] = act.astype(BF16)

            def shift_arr(step):
                store3(y3, 2 * step, arr[rows(2 * step, 2), :], 2)

            repeat(8, shift_arr)
            whole[rows(0, 4), :] = hid_e[rows(0, 4), :]
            whole[rows(4, 10), :] = hid_m[...]
            whole[rows(14, 4), :] = hid_e[rows(4, 4), :]

            def second_grad(a):
                put_grad(grad, 1, a, outer(whole[rows(a, 16), :], y3[...]))

            def first_grad(a):
                put_grad(grad, 0, a, outer(whole[rows(a, 16), :], z3[...]))

            repeat(3, second_grad)
            fill3(z3, 0, act_e, 1, 3)
            fill3(z3, 3, act_m, 0, 10)
            fill3(z3, 13, act_e, 4, 3)
            whole[rows(0, 1), :] = border[rows(0, 1), :]
            whole[rows(1, 16), :] = sta[...]
            whole[rows(17, 1), :] = border[rows(1, 1), :]
            repeat(3, first_grad)

    by_role(body)


def kernel_d(got_m, got_e, sta, hid_m, hid_e, slope_m, slope_e, grad_in, w, act2_e, grad, r3, z3, h6):
    def body(leading):
        fill3(r3, 0, got_e, 0, 4)
        fill3(r3, 4, got_m, 0, 2)
        fill3(r3, 6, got_m, 6, 2)
        fill3(r3, 8, got_e, 4, 4)
        total = conv(r3, (0, 6), 4, w, 1 if leading else 0, leading)
        if leading:
            slope = jnp.concatenate(
                [
                    slope_e[rows(2, 2), :],
                    slope_m[rows(0, 2), :],
                    slope_m[rows(8, 2), :],
                    slope_e[rows(4, 2), :],
                ],
                axis=0,
            )
            act = total * slope.astype(F32)
            store3(z3, 0, act, 8)
        else:
            act, _ = activate(total)
        act2_e[...] = act.astype(BF16)
        if leading:
            h6[rows(0, 4), :] = hid_e[rows(0, 4), :]
            h6[rows(4, 2), :] = hid_m[rows(0, 2), :]
            h6[rows(6, 2), :] = hid_m[rows(8, 2), :]
            h6[rows(8, 4), :] = hid_e[rows(4, 4), :]
            for a in range(3):
                more = outer(h6[rows(a, 4), :], r3[rows(0, 4), :])
                more = more + outer(h6[rows(6 + a, 4), :], r3[rows(8, 4), :])
                put_grad(grad, 1, a, get_grad(grad_in, 1, a) + more)
                more = outer(sta[rows(a, 4), :], z3[rows(0, 4), :])
                more = more + outer(sta[rows(10 + a, 4), :], z3[rows(4, 4), :])
                put_grad(grad, 0, a, get_grad(grad_in, 0, a) + more)

    by_role(body)


def kernel_e(
    scale, got_e, got_near, got_far, sta, border, slope_e, grad_c, grad_d, w, act2_h, send, keep, r3, z3, x2, tot
):
    has_up, has_down = edge_flags()
    core = lax.axis_index("space_2")

    def emit(src, from_at, to_at, width):
        for pair in range(8):
            for dst, side in ((keep, core), (send, 1 - core)):
                first = pl.multiple_of(32 * pair + 8 * side, 8)
                second = pl.multiple_of(32 * pair + 16 + 8 * side, 8)
                val = jnp.concatenate(
                    [
                        src[pl.ds(first, 8), from_at : from_at + width],
                        src[pl.ds(second, 8), from_at : from_at + width],
                    ],
                    axis=0,
                )
                dst[pl.ds(16 * pair, 16), to_at : to_at + width] = (val * scale).astype(dst.dtype)

    def body(leading):
        store3(r3, 0, above(got_near[...], got_far[...]), 2)
        fill3(r3, 2, got_e, 0, 2)
        fill3(r3, 4, got_e, 6, 2)
        store3(r3, 6, below(got_near[...], got_far[...]), 2)
        spot = lax.broadcasted_iota(jnp.int32, (4 * COLS, CH), 0) // COLS
        total = conv(r3, (0, 4), 2, w, 1 if leading else 0, leading)
        if leading:
            slope = jnp.concatenate([slope_e[rows(0, 2), :], slope_e[rows(6, 2), :]], axis=0)
            act = total * slope.astype(F32)
        else:
            act, _ = activate(total)
        act = act * jnp.where(spot == 0, has_up, jnp.where(spot == 3, has_down, 1.0))
        act2_h[...] = act.astype(BF16)
        if leading:
            store3(z3, 0, act2_h[rows(1, 2), :], 2)
            x2[rows(0, 1), :] = border[rows(0, 1), :]
            x2[rows(1, 2), :] = sta[rows(0, 2), :]
            x2[rows(3, 2), :] = sta[rows(14, 2), :]
            x2[rows(5, 1), :] = border[rows(1, 1), :]
            for a in range(3):
                left = jnp.concatenate([x2[rows(a, 1), :], x2[rows(3 + a, 1), :]], axis=0)
                put_grad(tot, 0, a, get_grad(grad_d, 0, a) + outer(left, z3[...]))
            emit(tot, 0, 0, TAPS)
            emit(grad_d, TAPS, TAPS, TAPS)
        else:
            emit(grad_c, 0, 0, 2 * TAPS)

    by_role(body)


def kernel_pick(got_e, inner, outer):
    core = lax.axis_index("space_2")
    inner[...] = got_e[rows(6 * (1 - core), 2), :]
    outer[...] = got_e[rows(6 * core, 2), :]


def kernel_sum(keep, other, total):
    for row in range(0, keep.shape[0], 16):
        part = pl.ds(row, 16)
        total[part, :] = (keep[part, :] + other[part, :].astype(F32)).astype(BF16)


def kernel_f(got_m, got_e, act2_m, act2_e, act2_h, w, out, c3, kept):
    def body(leading):
        fill3(c3, 0, act2_h, 0, 2)
        fill3(c3, 2, act2_e, 0, 4)
        fill3(c3, 6, act2_m, 0, 6)
        fill3(c3, 12, act2_e, 4, 4)
        fill3(c3, 16, act2_h, 2, 2)
        kept[rows(0, 4), :] = got_e[rows(0, 4), :]
        kept[rows(4, 8), :] = got_m[...]
        kept[rows(12, 4), :] = got_e[rows(4, 4), :]

        def block(step):
            row = 4 * step
            total = conv(c3, row, 4, w, 0 if leading else 1, leading)
            out[rows(row, 4), :] = (total + kept[rows(row, 4), :].astype(F32)).astype(BF16)

        repeat(4, block)

    by_role(body)


def call(body, outs, scratch, args, row_units, limit=18, space=pltpu.VMEM, sems=0):
    block = pl.BlockSpec(memory_space=pltpu.VMEM)
    semaphores = [pltpu.SemaphoreType.DMA((sems,))] if sems else []
    return pl.pallas_call(
        body,
        out_shape=[jax.ShapeDtypeStruct(shape, dtype) for shape, dtype in outs],
        in_specs=[pl.BlockSpec(memory_space=space)] * len(args),
        out_specs=[block] * len(outs),
        scratch_shapes=[pltpu.VMEM(shape, dtype) for shape, dtype in scratch] + semaphores,
        compiler_params=pltpu.CompilerParams(vmem_limit_bytes=limit * MIB),
        cost_estimate=pl.CostEstimate(
            flops=int(row_units * 2 * COLS * TAPS * CH),
            bytes_accessed=4 * MIB,
            transcendentals=0,
        ),
    )(*args)


def tick(arrivals, stashed, weights):
    arr = arrivals.reshape(-1, CH)
    sta = stashed.reshape(-1, CH)
    w = weights[0, 0]
    tile = arr.shape[0] // COLS
    space = lax.axis_size(SPACE)
    scale = 1.0 / math.sqrt(tile * space * COLS)

    def img(count, dtype=BF16):
        return ((count * COLS, CH), dtype)

    def img3(count):
        return ((count * COLS, 3 * CH), BF16)

    grad_shape = ((CH, 2 * TAPS), F32)

    two = 2 * COLS
    edge = ((2, two, CH), BF16)
    out_m, act_m, hid_m, slope_m, near, far, sta_v = call(
        kernel_a,
        [img(8), img(10), img(10), img(10), edge, edge, img(16)],
        [img3(12), img3(12), img3(10), (w.shape, BF16), img(16), img(10, F32)],
        (arr, sta, w),
        28,
        limit=LIMIT_A,
        space=pltpu.HBM,
        sems=8,
    )
    sta = sta_v
    hop = [(i, i + 1) for i in range(1, space - 1, 2)]
    hop = hop + [(j, i) for i, j in hop]
    swap = [(0, 1), (1, 0)]
    got_m = lax.ppermute(out_m, "segment", swap)
    near = lax.ppermute(near, "space_2", swap)
    far = lax.ppermute(far, SPACE, hop)
    quad = call(
        kernel_q,
        [img(4), img(4), img(4), img(4)],
        [img3(8), img3(8), img3(8), img(4, F32)],
        (arr, sta, act_m, w),
        12,
    )
    out_e, act_e, hid_e, slope_e, border = call(
        kernel_b,
        [img(8), img(8), img(8), img(8), img(2)],
        [img3(8), img3(8), img3(8), img(4, F32)],
        (arr, sta, near, far, *quad, w),
        12,
    )
    got_e = lax.ppermute(out_e, "segment", swap)
    inner_rows, outer_rows = call(kernel_pick, [img(2), img(2)], [], (got_e,), 0, limit=4)
    got_near = lax.ppermute(inner_rows, "space_2", swap)
    got_far = lax.ppermute(outer_rows, SPACE, hop)
    act2_m, grad_c = call(
        kernel_c,
        [img(6), grad_shape],
        [img3(8), img3(16), img3(16), img(18)],
        (got_m, arr, sta, border, act_m, act_e, hid_m, hid_e, slope_m, w),
        38,
    )
    act2_e, grad_d = call(
        kernel_d,
        [img(8), grad_shape],
        [img3(12), img3(8), img(12)],
        (got_m, got_e, sta, hid_m, hid_e, slope_m, slope_e, grad_c, w),
        24,
    )
    act2_h, sent, keep = call(
        functools.partial(kernel_e, scale),
        [img(4), ((CH // 2, 2 * TAPS), BF16), ((CH // 2, 2 * TAPS), F32)],
        [img3(8), img3(2), img(6), ((CH, TAPS), F32)],
        (got_e, got_near, got_far, sta, border, slope_e, grad_c, grad_d, w),
        8,
    )
    (departing,) = call(
        kernel_f, [img(16)], [img3(18), img(16)], (got_m, got_e, act2_m, act2_e, act2_h, w), 16
    )

    chips = space // 2
    share = CH // space
    other = lax.ppermute(sent, "space_2", swap)
    (pieces,) = call(kernel_sum, [(keep.shape, BF16)], [], (keep, other), 0, limit=8)
    pieces = pieces.reshape(chips, share, 2 * TAPS)
    pieces = lax.all_to_all(pieces, ("space_0", "space_1"), 0, 0, tiled=True)
    owned = jnp.sum(pieces.astype(F32), axis=0)
    owned, departing = lax.optimization_barrier((owned, departing))
    pairs = [(i, i ^ 3) for i in range(4)]
    partner = lax.ppermute(owned.astype(BF16), ("segment", "mirror"), pairs)
    combined = owned + partner.astype(F32)
    return (
        departing.reshape(arrivals.shape),
        combined.reshape(1, 1, share, 2, 3, 3, CH),
    )


def solution(mesh):
    split = Mesh(
        mesh.devices.reshape(mesh.shape["segment"], 4, 4, 2, mesh.shape["mirror"]),
        ("segment", "space_0", "space_1", "space_2", "mirror"),
    )
    in_specs = (
        P("mirror", "segment", SPACE, None, None),
        P("mirror", "segment", SPACE, None, None),
        P("mirror", "segment", None, None, None, None, None),
    )
    out_specs = (
        P("mirror", "segment", SPACE, None, None),
        P("mirror", "segment", SPACE, None, None, None, None),
    )
    return jax.shard_map(tick, mesh=split, in_specs=in_specs, out_specs=out_specs, check_vma=False)
```

```python
import functools
import math

import jax
import jax.numpy as jnp
from jax import lax
from jax.experimental import pallas as pl
from jax.experimental.pallas import tpu as pltpu
from jax.sharding import Mesh
from jax.sharding import PartitionSpec as P

SPACE = ("space_0", "space_1", "space_2")
BF16 = jnp.bfloat16
F32 = jnp.float32
COLS = 128
CH = 256
TAPS = 9 * CH
MIB = 1 << 20
LIMIT_A = 50
LIMIT_B = 55


def rows(first, count):
    start = first * COLS
    if not isinstance(start, int):
        start = pl.multiple_of(start, COLS)
    return pl.ds(start, count * COLS)


def repeat(steps, body):
    def step(index, carry):
        body(index)
        return carry

    lax.fori_loop(0, steps, step, 0)


def store3(dst, row, val, count):
    size = count * COLS
    col = lax.broadcasted_iota(jnp.int32, (size, CH), 0) & (COLS - 1)
    val = val.astype(F32)
    left = jnp.where(col == 0, 0.0, pltpu.roll(val, 1, 0))
    right = jnp.where(col == COLS - 1, 0.0, pltpu.roll(val, size - 1, 0))
    where = rows(row, count)
    dst[where, 0:CH] = left.astype(BF16)
    dst[where, CH : 2 * CH] = val.astype(BF16)
    dst[where, 2 * CH :] = right.astype(BF16)


def fill3(dst, row, src, first, count):
    for step in range(0, count, 2):
        size = min(2, count - step)
        store3(dst, row + step, src[rows(first + step, size), :], size)


def conv(src3, first, count, weights, which, transposed):
    firsts = first if isinstance(first, tuple) else (first,)
    total = None
    for a in range(3):
        for b in range(3):
            parts = [src3[rows(at + a, count), b * CH : (b + 1) * CH] for at in firsts]
            window = parts[0] if len(parts) == 1 else jnp.concatenate(parts, axis=0)
            if transposed:
                part = lax.dot_general(
                    window,
                    weights[which, 2 - a, 2 - b],
                    (((1,), (1,)), ((), ())),
                    preferred_element_type=F32,
                )
            else:
                part = jnp.dot(window, weights[which, a, b], preferred_element_type=F32)
            total = part if total is None else total + part
    return total


def outer(left, right):
    return lax.dot_general(left, right, (((0,), (0,)), ((), ())), preferred_element_type=F32)


def put_grad(dst, conv_index, a, val):
    for b in range(3):
        at = conv_index * TAPS + (3 * a + b) * CH
        if not isinstance(at, int):
            at = pl.multiple_of(at, CH)
        dst[:, pl.ds(at, CH)] = val[:, (2 - b) * CH : (3 - b) * CH]


def get_grad(src, conv_index, a):
    parts = []
    for b in (2, 1, 0):
        at = conv_index * TAPS + (3 * a + b) * CH
        parts.append(src[:, at : at + CH])
    return jnp.concatenate(parts, axis=1)


def activate(pre):
    sig = jax.nn.sigmoid(pre)
    return pre * sig, sig * (1.0 + pre * (1.0 - sig))


def is_leading():
    return lax.axis_index("segment") == lax.axis_index("mirror")


def by_role(body):
    leading = is_leading()

    @pl.when(leading)
    def _():
        body(True)

    @pl.when(jnp.logical_not(leading))
    def _():
        body(False)


def edge_flags():
    place = lax.axis_index(SPACE)
    count = lax.axis_size(SPACE)
    return (place > 0).astype(F32), (place < count - 1).astype(F32)


def above(near, far):
    return jnp.where(lax.axis_index("space_2") == 1, near.astype(F32), far.astype(F32))


def below(near, far):
    return jnp.where(lax.axis_index("space_2") == 0, near.astype(F32), far.astype(F32))


def kernel_edges(arr_hbm, sta_hbm, near, far, sems):
    two = 2 * COLS
    size = arr_hbm.shape[0]
    core = lax.axis_index("space_2")
    inner_at = pl.ds(pl.multiple_of((1 - core) * (size - two), two), two)
    outer_at = pl.ds(pl.multiple_of(core * (size - two), two), two)
    moves = (
        (arr_hbm.at[inner_at], near.at[0]),
        (sta_hbm.at[inner_at], near.at[1]),
        (arr_hbm.at[outer_at], far.at[0]),
        (sta_hbm.at[outer_at], far.at[1]),
    )
    copies = [pltpu.make_async_copy(src, dst, sems.at[i]) for i, (src, dst) in enumerate(moves)]
    for copy in copies:
        copy.start()
    for copy in copies:
        copy.wait()


def kernel_a(arr_hbm, sta_hbm, w_hbm, out_m, act_m, hid_m, slope_m, sta, s3, a3, c3, w, arr, steep, sems):
    moves = (
        (sta_hbm, sta),
        (w_hbm.at[0], w.at[0]),
        (arr_hbm, arr),
        (w_hbm.at[1], w.at[1]),
    )
    copies = [pltpu.make_async_copy(src, dst, sems.at[i]) for i, (src, dst) in enumerate(moves)]
    for copy in copies:
        copy.start()
    for copy in copies[:2]:
        copy.wait()
    fill3(s3, 0, sta, 2, 12)
    for row in (0, 5):
        hid, slope = activate(conv(s3, row, 5, w, 0, False))
        hid_m[rows(row, 5), :] = hid.astype(BF16)
        slope_m[rows(row, 5), :] = slope.astype(BF16)
        steep[rows(row, 5), :] = slope
    for copy in copies[2:]:
        copy.wait()

    def body(leading):
        fill3(a3, 0, arr, 2, 12)
        for row in (0, 5):
            if leading:
                act, _ = activate(conv(a3, row, 5, w, 0, False))
            else:
                act = conv(a3, row, 5, w, 1, True) * steep[rows(row, 5), :]
            act_m[rows(row, 5), :] = act.astype(BF16)
            store3(c3, row, act, 5)
        for row in (0, 4):
            total = conv(c3, row, 4, w, 1 if leading else 0, not leading)
            out_m[rows(row, 4), :] = (total + arr[rows(4 + row, 4), :].astype(F32)).astype(BF16)

    by_role(body)


def kernel_q(arr, sta, act_m, w, out_q, act_q, hid_q, slope_q, s3, a3, c3, steep):
    fill3(s3, 0, sta, 0, 4)
    fill3(s3, 4, sta, 12, 4)
    hid, slope = activate(conv(s3, (0, 4), 2, w, 0, False))
    hid_q[...] = hid.astype(BF16)
    slope_q[...] = slope.astype(BF16)
    steep[...] = slope

    def body(leading):
        fill3(a3, 0, arr, 0, 4)
        fill3(a3, 4, arr, 12, 4)
        fill3(c3, 2, act_m, 0, 2)
        fill3(c3, 4, act_m, 8, 2)
        if leading:
            act, _ = activate(conv(a3, (0, 4), 2, w, 0, False))
        else:
            act = conv(a3, (0, 4), 2, w, 1, True) * steep[...]
        act_q[...] = act.astype(BF16)
        store3(c3, 0, act[: 2 * COLS], 2)
        store3(c3, 6, act[2 * COLS :], 2)
        total = conv(c3, (0, 4), 2, w, 1 if leading else 0, not leading)
        for half in range(2):
            kept = arr[rows(2 + 10 * half, 2), :].astype(F32)
            out_q[rows(2 * half, 2), :] = (total[2 * half * COLS : (2 * half + 2) * COLS] + kept).astype(BF16)

    by_role(body)


def kernel_b(
    arr, sta, near, far, out_q, act_q, hid_q, slope_q, w, out_e, act_e, hid_e, slope_e, border, s3, a3, c3, steep
):
    has_up, has_down = edge_flags()

    def spread(dst, mid, val):
        val = val.astype(BF16)
        dst[rows(0, 2), :] = val[: 2 * COLS]
        dst[rows(2, 4), :] = mid[...]
        dst[rows(6, 2), :] = val[2 * COLS :]

    up, down = above(near[1], far[1]), below(near[1], far[1])
    border[rows(0, 1), :] = up[COLS:].astype(BF16)
    border[rows(1, 1), :] = down[:COLS].astype(BF16)
    store3(s3, 0, up, 2)
    fill3(s3, 2, sta, 0, 2)
    fill3(s3, 4, sta, 14, 2)
    store3(s3, 6, down, 2)
    spot = lax.broadcasted_iota(jnp.int32, (4 * COLS, CH), 0) // COLS
    mask = jnp.where(spot == 0, has_up, jnp.where(spot == 3, has_down, 1.0))
    hid, slope = activate(conv(s3, (0, 4), 2, w, 0, False))
    spread(hid_e, hid_q, hid * mask)
    spread(slope_e, slope_q, slope)
    steep[...] = slope * mask

    def body(leading):
        store3(a3, 0, above(near[0], far[0]), 2)
        fill3(a3, 2, arr, 0, 2)
        fill3(a3, 4, arr, 14, 2)
        store3(a3, 6, below(near[0], far[0]), 2)
        fill3(c3, 2, act_q, 0, 2)
        fill3(c3, 4, act_q, 2, 2)
        if leading:
            act, _ = activate(conv(a3, (0, 4), 2, w, 0, False))
            spot = lax.broadcasted_iota(jnp.int32, (4 * COLS, CH), 0) // COLS
            act = act * jnp.where(spot == 0, has_up, jnp.where(spot == 3, has_down, 1.0))
        else:
            act = conv(a3, (0, 4), 2, w, 1, True) * steep[...]
        spread(act_e, act_q, act)
        store3(c3, 0, act[: 2 * COLS], 2)
        store3(c3, 6, act[2 * COLS :], 2)
        total = conv(c3, (0, 4), 2, w, 1 if leading else 0, not leading)
        for half in range(2):
            kept = arr[rows(14 * half, 2), :].astype(F32)
            part = total[2 * half * COLS : (2 * half + 2) * COLS] + kept
            out_e[rows(6 * half, 2), :] = part.astype(BF16)
        out_e[rows(2, 4), :] = out_q[...]

    by_role(body)


def kernel_c(
    got_m, arr, sta, border, act_m, act_e, hid_m, hid_e, slope_m, w, act2_m, grad, r3, y3, z3, whole
):
    def body(leading):
        fill3(r3, 0, got_m, 0, 8)
        total = conv(r3, 0, 6, w, 1 if leading else 0, leading)
        if leading:
            act = total * slope_m[rows(2, 6), :].astype(F32)
            act2_m[...] = act.astype(BF16)
            store3(z3, 0, act, 6)
            for a in range(3):
                put_grad(grad, 1, a, outer(hid_m[rows(a, 8), :], r3[rows(0, 8), :]))
                put_grad(grad, 0, a, outer(sta[rows(4 + a, 6), :], z3[rows(0, 6), :]))
        else:
            act, _ = activate(total)
            act2_m[...] = act.astype(BF16)

            def shift_arr(step):
                store3(y3, 2 * step, arr[rows(2 * step, 2), :], 2)

            repeat(8, shift_arr)
            whole[rows(0, 4), :] = hid_e[rows(0, 4), :]
            whole[rows(4, 10), :] = hid_m[...]
            whole[rows(14, 4), :] = hid_e[rows(4, 4), :]

            def second_grad(a):
                put_grad(grad, 1, a, outer(whole[rows(a, 16), :], y3[...]))

            def first_grad(a):
                put_grad(grad, 0, a, outer(whole[rows(a, 16), :], z3[...]))

            repeat(3, second_grad)
            fill3(z3, 0, act_e, 1, 3)
            fill3(z3, 3, act_m, 0, 10)
            fill3(z3, 13, act_e, 4, 3)
            whole[rows(0, 1), :] = border[rows(0, 1), :]
            whole[rows(1, 16), :] = sta[...]
            whole[rows(17, 1), :] = border[rows(1, 1), :]
            repeat(3, first_grad)

    by_role(body)


def kernel_d(got_m, got_e, sta, hid_m, hid_e, slope_m, slope_e, grad_in, w, act2_e, grad, r3, z3, h6):
    def body(leading):
        fill3(r3, 0, got_e, 0, 4)
        fill3(r3, 4, got_m, 0, 2)
        fill3(r3, 6, got_m, 6, 2)
        fill3(r3, 8, got_e, 4, 4)
        for half in range(2):
            total = conv(r3, 6 * half, 4, w, 1 if leading else 0, leading)
            if leading:
                if half == 0:
                    slope = jnp.concatenate([slope_e[rows(2, 2), :], slope_m[rows(0, 2), :]], axis=0)
                else:
                    slope = jnp.concatenate([slope_m[rows(8, 2), :], slope_e[rows(4, 2), :]], axis=0)
                act = total * slope.astype(F32)
                store3(z3, 4 * half, act, 4)
            else:
                act, _ = activate(total)
            act2_e[rows(4 * half, 4), :] = act.astype(BF16)
        if leading:
            h6[rows(0, 4), :] = hid_e[rows(0, 4), :]
            h6[rows(4, 2), :] = hid_m[rows(0, 2), :]
            h6[rows(6, 2), :] = hid_m[rows(8, 2), :]
            h6[rows(8, 4), :] = hid_e[rows(4, 4), :]
            for a in range(3):
                more = outer(h6[rows(a, 4), :], r3[rows(0, 4), :])
                more = more + outer(h6[rows(6 + a, 4), :], r3[rows(8, 4), :])
                put_grad(grad, 1, a, get_grad(grad_in, 1, a) + more)
                more = outer(sta[rows(a, 4), :], z3[rows(0, 4), :])
                more = more + outer(sta[rows(10 + a, 4), :], z3[rows(4, 4), :])
                put_grad(grad, 0, a, get_grad(grad_in, 0, a) + more)

    by_role(body)


def kernel_e(
    scale, got_e, got_near, got_far, sta, border, slope_e, grad_c, grad_d, w, act2_h, send, keep, r3, z3, x2, tot
):
    has_up, has_down = edge_flags()
    core = lax.axis_index("space_2")

    def emit(src, from_at, to_at, width):
        for pair in range(8):
            for dst, side in ((keep, core), (send, 1 - core)):
                first = pl.multiple_of(32 * pair + 8 * side, 8)
                second = pl.multiple_of(32 * pair + 16 + 8 * side, 8)
                val = jnp.concatenate(
                    [
                        src[pl.ds(first, 8), from_at : from_at + width],
                        src[pl.ds(second, 8), from_at : from_at + width],
                    ],
                    axis=0,
                )
                dst[pl.ds(16 * pair, 16), to_at : to_at + width] = (val * scale).astype(dst.dtype)

    def body(leading):
        store3(r3, 0, above(got_near[...], got_far[...]), 2)
        fill3(r3, 2, got_e, 0, 2)
        fill3(r3, 4, got_e, 6, 2)
        store3(r3, 6, below(got_near[...], got_far[...]), 2)
        spot = lax.broadcasted_iota(jnp.int32, (2 * COLS, CH), 0) // COLS
        for half in range(2):
            total = conv(r3, 4 * half, 2, w, 1 if leading else 0, leading)
            if leading:
                act = total * slope_e[rows(6 * half, 2), :].astype(F32)
            else:
                act, _ = activate(total)
            if half == 0:
                act = act * jnp.where(spot == 0, has_up, 1.0)
            else:
                act = act * jnp.where(spot == 1, has_down, 1.0)
            act2_h[rows(2 * half, 2), :] = act.astype(BF16)
        if leading:
            store3(z3, 0, act2_h[rows(1, 2), :], 2)
            x2[rows(0, 1), :] = border[rows(0, 1), :]
            x2[rows(1, 2), :] = sta[rows(0, 2), :]
            x2[rows(3, 2), :] = sta[rows(14, 2), :]
            x2[rows(5, 1), :] = border[rows(1, 1), :]
            for a in range(3):
                left = jnp.concatenate([x2[rows(a, 1), :], x2[rows(3 + a, 1), :]], axis=0)
                put_grad(tot, 0, a, get_grad(grad_d, 0, a) + outer(left, z3[...]))
            emit(tot, 0, 0, TAPS)
            emit(grad_d, TAPS, TAPS, TAPS)
        else:
            emit(grad_c, 0, 0, 2 * TAPS)

    by_role(body)


def kernel_pick(got_e, inner, outer):
    core = lax.axis_index("space_2")
    inner[...] = got_e[rows(6 * (1 - core), 2), :]
    outer[...] = got_e[rows(6 * core, 2), :]


def kernel_sum(keep, other, total):
    for row in range(0, keep.shape[0], 16):
        part = pl.ds(row, 16)
        total[part, :] = (keep[part, :] + other[part, :].astype(F32)).astype(BF16)


def kernel_f(got_m, got_e, act2_m, act2_e, act2_h, w, out, c3, kept):
    def body(leading):
        fill3(c3, 0, act2_h, 0, 2)
        fill3(c3, 2, act2_e, 0, 4)
        fill3(c3, 6, act2_m, 0, 6)
        fill3(c3, 12, act2_e, 4, 4)
        fill3(c3, 16, act2_h, 2, 2)
        kept[rows(0, 4), :] = got_e[rows(0, 4), :]
        kept[rows(4, 8), :] = got_m[...]
        kept[rows(12, 4), :] = got_e[rows(4, 4), :]

        def block(step):
            row = 4 * step
            total = conv(c3, row, 4, w, 0 if leading else 1, leading)
            out[rows(row, 4), :] = (total + kept[rows(row, 4), :].astype(F32)).astype(BF16)

        repeat(4, block)

    by_role(body)


def call(body, outs, scratch, args, row_units, limit=18, space=pltpu.VMEM, sems=0):
    block = pl.BlockSpec(memory_space=pltpu.VMEM)
    semaphores = [pltpu.SemaphoreType.DMA((sems,))] if sems else []
    return pl.pallas_call(
        body,
        out_shape=[jax.ShapeDtypeStruct(shape, dtype) for shape, dtype in outs],
        in_specs=[pl.BlockSpec(memory_space=space)] * len(args),
        out_specs=[block] * len(outs),
        scratch_shapes=[pltpu.VMEM(shape, dtype) for shape, dtype in scratch] + semaphores,
        compiler_params=pltpu.CompilerParams(vmem_limit_bytes=limit * MIB),
        cost_estimate=pl.CostEstimate(
            flops=int(row_units * 2 * COLS * TAPS * CH),
            bytes_accessed=4 * MIB,
            transcendentals=0,
        ),
    )(*args)


def tick(arrivals, stashed, weights):
    arr = arrivals.reshape(-1, CH)
    sta = stashed.reshape(-1, CH)
    w = weights[0, 0]
    tile = arr.shape[0] // COLS
    space = lax.axis_size(SPACE)
    scale = 1.0 / math.sqrt(tile * space * COLS)

    def img(count, dtype=BF16):
        return ((count * COLS, CH), dtype)

    def img3(count):
        return ((count * COLS, 3 * CH), BF16)

    grad_shape = ((CH, 2 * TAPS), F32)

    two = 2 * COLS
    edge = ((2, two, CH), BF16)
    near, far = call(
        kernel_edges, [edge, edge], [], (arr, sta), 0, limit=LIMIT_B, space=pltpu.HBM, sems=4
    )
    hop = [(i, i + 1) for i in range(1, space - 1, 2)]
    hop = hop + [(j, i) for i, j in hop]
    swap = [(0, 1), (1, 0)]
    near = lax.ppermute(near, "space_2", swap)
    far = lax.ppermute(far, SPACE, hop)
    out_m, act_m, hid_m, slope_m, sta = call(
        kernel_a,
        [img(8), img(10), img(10), img(10), img(16)],
        [img3(12), img3(12), img3(10), (w.shape, BF16), img(16), img(10, F32)],
        (arr, sta, w),
        28,
        limit=LIMIT_A,
        space=pltpu.HBM,
        sems=4,
    )
    got_m = lax.ppermute(out_m, "segment", swap)
    quad = call(
        kernel_q,
        [img(4), img(4), img(4), img(4)],
        [img3(8), img3(8), img3(8), img(4, F32)],
        (arr, sta, act_m, w),
        12,
    )
    out_e, act_e, hid_e, slope_e, border = call(
        kernel_b,
        [img(8), img(8), img(8), img(8), img(2)],
        [img3(8), img3(8), img3(8), img(4, F32)],
        (arr, sta, near, far, *quad, w),
        12,
    )
    got_e = lax.ppermute(out_e, "segment", swap)
    inner_rows, outer_rows = call(kernel_pick, [img(2), img(2)], [], (got_e,), 0, limit=4)
    got_near = lax.ppermute(inner_rows, "space_2", swap)
    got_far = lax.ppermute(outer_rows, SPACE, hop)
    act2_m, grad_c = call(
        kernel_c,
        [img(6), grad_shape],
        [img3(8), img3(16), img3(16), img(18)],
        (got_m, arr, sta, border, act_m, act_e, hid_m, hid_e, slope_m, w),
        38,
    )
    act2_e, grad_d = call(
        kernel_d,
        [img(8), grad_shape],
        [img3(12), img3(8), img(12)],
        (got_m, got_e, sta, hid_m, hid_e, slope_m, slope_e, grad_c, w),
        24,
    )
    act2_h, sent, keep = call(
        functools.partial(kernel_e, scale),
        [img(4), ((CH // 2, 2 * TAPS), BF16), ((CH // 2, 2 * TAPS), F32)],
        [img3(8), img3(2), img(6), ((CH, TAPS), F32)],
        (got_e, got_near, got_far, sta, border, slope_e, grad_c, grad_d, w),
        8,
    )
    (departing,) = call(
        kernel_f, [img(16)], [img3(18), img(16)], (got_m, got_e, act2_m, act2_e, act2_h, w), 16
    )

    chips = space // 2
    share = CH // space
    other = lax.ppermute(sent, "space_2", swap)
    (pieces,) = call(kernel_sum, [(keep.shape, BF16)], [], (keep, other), 0, limit=8)
    pieces = pieces.reshape(chips, share, 2 * TAPS)
    pieces = lax.all_to_all(pieces, ("space_0", "space_1"), 0, 0, tiled=True)
    owned = jnp.sum(pieces.astype(F32), axis=0)
    owned, departing = lax.optimization_barrier((owned, departing))
    pairs = [(i, i ^ 3) for i in range(4)]
    partner = lax.ppermute(owned.astype(BF16), ("segment", "mirror"), pairs)
    combined = owned + partner.astype(F32)
    return (
        departing.reshape(arrivals.shape),
        combined.reshape(1, 1, share, 2, 3, 3, CH),
    )


def solution(mesh):
    split = Mesh(
        mesh.devices.reshape(mesh.shape["segment"], 4, 4, 2, mesh.shape["mirror"]),
        ("segment", "space_0", "space_1", "space_2", "mirror"),
    )
    in_specs = (
        P("mirror", "segment", SPACE, None, None),
        P("mirror", "segment", SPACE, None, None),
        P("mirror", "segment", None, None, None, None, None),
    )
    out_specs = (
        P("mirror", "segment", SPACE, None, None),
        P("mirror", "segment", SPACE, None, None, None, None),
    )
    return jax.shard_map(tick, mesh=split, in_specs=in_specs, out_specs=out_specs, check_vma=False)
```

```python
import functools
import math

import jax
import jax.numpy as jnp
from jax import lax
from jax.experimental import pallas as pl
from jax.experimental.pallas import tpu as pltpu
from jax.sharding import Mesh
from jax.sharding import PartitionSpec as P

SPACE = ("space_0", "space_1", "space_2")
BF16 = jnp.bfloat16
F32 = jnp.float32
COLS = 128
CH = 256
TAPS = 9 * CH
MIB = 1 << 20
LIMIT_A = 49


def rows(first, count):
    start = first * COLS
    if not isinstance(start, int):
        start = pl.multiple_of(start, COLS)
    return pl.ds(start, count * COLS)


def repeat(steps, body):
    def step(index, carry):
        body(index)
        return carry

    lax.fori_loop(0, steps, step, 0)


def store3(dst, row, val, count):
    size = count * COLS
    col = lax.broadcasted_iota(jnp.int32, (size, CH), 0) & (COLS - 1)
    val = val.astype(F32)
    left = jnp.where(col == 0, 0.0, pltpu.roll(val, 1, 0))
    right = jnp.where(col == COLS - 1, 0.0, pltpu.roll(val, size - 1, 0))
    where = rows(row, count)
    dst[where, 0:CH] = left.astype(BF16)
    dst[where, CH : 2 * CH] = val.astype(BF16)
    dst[where, 2 * CH :] = right.astype(BF16)


def fill3(dst, row, src, first, count):
    for step in range(0, count, 2):
        size = min(2, count - step)
        store3(dst, row + step, src[rows(first + step, size), :], size)


def conv(src3, first, count, weights, which, transposed):
    firsts = first if isinstance(first, tuple) else (first,)
    total = None
    for a in range(3):
        for b in range(3):
            parts = [src3[rows(at + a, count), b * CH : (b + 1) * CH] for at in firsts]
            window = parts[0] if len(parts) == 1 else jnp.concatenate(parts, axis=0)
            if transposed:
                part = lax.dot_general(
                    window,
                    weights[which, 2 - a, 2 - b],
                    (((1,), (1,)), ((), ())),
                    preferred_element_type=F32,
                )
            else:
                part = jnp.dot(window, weights[which, a, b], preferred_element_type=F32)
            total = part if total is None else total + part
    return total


def outer(left, right):
    return lax.dot_general(left, right, (((0,), (0,)), ((), ())), preferred_element_type=F32)


def put_grad(dst, conv_index, a, val):
    for b in range(3):
        at = conv_index * TAPS + (3 * a + b) * CH
        if not isinstance(at, int):
            at = pl.multiple_of(at, CH)
        dst[:, pl.ds(at, CH)] = val[:, (2 - b) * CH : (3 - b) * CH]


def get_grad(src, conv_index, a):
    parts = []
    for b in (2, 1, 0):
        at = conv_index * TAPS + (3 * a + b) * CH
        parts.append(src[:, at : at + CH])
    return jnp.concatenate(parts, axis=1)


def activate(pre):
    sig = jax.nn.sigmoid(pre)
    return pre * sig, sig * (1.0 + pre * (1.0 - sig))


def is_leading():
    return lax.axis_index("segment") == lax.axis_index("mirror")


def by_role(body):
    leading = is_leading()

    @pl.when(leading)
    def _():
        body(True)

    @pl.when(jnp.logical_not(leading))
    def _():
        body(False)


def edge_flags():
    place = lax.axis_index(SPACE)
    count = lax.axis_size(SPACE)
    return (place > 0).astype(F32), (place < count - 1).astype(F32)


def above(near, far):
    return jnp.where(lax.axis_index("space_2") == 1, near.astype(F32), far.astype(F32))


def below(near, far):
    return jnp.where(lax.axis_index("space_2") == 0, near.astype(F32), far.astype(F32))


def kernel_a(
    arr_hbm, sta_hbm, w_hbm, out_m, act_m, hid_m, slope_m, near, far, sta, s3, a3, c3, w, arr, steep, sems
):
    two = 2 * COLS
    size = arr_hbm.shape[0]
    core = lax.axis_index("space_2")
    inner_at = pl.ds(pl.multiple_of((1 - core) * (size - two), two), two)
    outer_at = pl.ds(pl.multiple_of(core * (size - two), two), two)
    moves = (
        (sta_hbm, sta),
        (w_hbm.at[0], w.at[0]),
        (arr_hbm, arr),
        (w_hbm.at[1], w.at[1]),
        (arr_hbm.at[inner_at], near.at[0]),
        (sta_hbm.at[inner_at], near.at[1]),
        (arr_hbm.at[outer_at], far.at[0]),
        (sta_hbm.at[outer_at], far.at[1]),
    )
    copies = [pltpu.make_async_copy(src, dst, sems.at[i]) for i, (src, dst) in enumerate(moves)]
    for copy in copies:
        copy.start()
    for copy in copies[:2]:
        copy.wait()
    fill3(s3, 0, sta, 0, 16)
    for row in (0, 7):
        hid, slope = activate(conv(s3, row, 7, w, 0, False))
        hid_m[rows(row, 7), :] = hid.astype(BF16)
        slope_m[rows(row, 7), :] = slope.astype(BF16)
        steep[rows(row, 7), :] = slope
    for copy in copies[2:]:
        copy.wait()

    def body(leading):
        fill3(a3, 0, arr, 0, 16)
        for row in (0, 7):
            if leading:
                act, _ = activate(conv(a3, row, 7, w, 0, False))
            else:
                act = conv(a3, row, 7, w, 1, True) * steep[rows(row, 7), :]
            act_m[rows(row, 7), :] = act.astype(BF16)
            store3(c3, row, act, 7)
        for row in (0, 6):
            total = conv(c3, row, 6, w, 1 if leading else 0, not leading)
            out_m[rows(row, 6), :] = (total + arr[rows(2 + row, 6), :].astype(F32)).astype(BF16)

    by_role(body)


def kernel_b(
    arr, sta, near, far, act_m, w, out_e, act_e, hid_e, slope_e, border, s3, a3, c3, steep
):
    has_up, has_down = edge_flags()

    up, down = above(near[1], far[1]), below(near[1], far[1])
    border[rows(0, 1), :] = up[COLS:].astype(BF16)
    border[rows(1, 1), :] = down[:COLS].astype(BF16)
    store3(s3, 0, up, 2)
    fill3(s3, 2, sta, 0, 2)
    fill3(s3, 4, sta, 14, 2)
    store3(s3, 6, down, 2)
    spot = lax.broadcasted_iota(jnp.int32, (4 * COLS, CH), 0) // COLS
    mask = jnp.where(spot == 0, has_up, jnp.where(spot == 3, has_down, 1.0))
    hid, slope = activate(conv(s3, (0, 4), 2, w, 0, False))
    hid_e[...] = (hid * mask).astype(BF16)
    slope_e[...] = slope.astype(BF16)
    steep[...] = slope * mask

    def body(leading):
        store3(a3, 0, above(near[0], far[0]), 2)
        fill3(a3, 2, arr, 0, 2)
        fill3(a3, 4, arr, 14, 2)
        store3(a3, 6, below(near[0], far[0]), 2)
        fill3(c3, 2, act_m, 0, 2)
        fill3(c3, 4, act_m, 12, 2)
        if leading:
            act, _ = activate(conv(a3, (0, 4), 2, w, 0, False))
            spot = lax.broadcasted_iota(jnp.int32, (4 * COLS, CH), 0) // COLS
            act = act * jnp.where(spot == 0, has_up, jnp.where(spot == 3, has_down, 1.0))
        else:
            act = conv(a3, (0, 4), 2, w, 1, True) * steep[...]
        act_e[...] = act.astype(BF16)
        store3(c3, 0, act[: 2 * COLS], 2)
        store3(c3, 6, act[2 * COLS :], 2)
        total = conv(c3, (0, 4), 2, w, 1 if leading else 0, not leading)
        for half in range(2):
            kept = arr[rows(14 * half, 2), :].astype(F32)
            part = total[2 * half * COLS : (2 * half + 2) * COLS] + kept
            out_e[rows(2 * half, 2), :] = part.astype(BF16)

    by_role(body)


def kernel_c(
    got_m, arr, sta, border, act_m, act_e, hid_m, hid_e, slope_m, w, act2_m, grad, r3, y3, z3, whole
):
    def body(leading):
        fill3(r3, 0, got_m, 0, 12)
        total = conv(r3, 0, 10, w, 1 if leading else 0, leading)
        if leading:
            act = total * slope_m[rows(2, 10), :].astype(F32)
            act2_m[...] = act.astype(BF16)
            store3(z3, 0, act, 10)
            for a in range(3):
                put_grad(grad, 1, a, outer(hid_m[rows(a, 12), :], r3[...]))
                put_grad(grad, 0, a, outer(sta[rows(2 + a, 10), :], z3[rows(0, 10), :]))
        else:
            act, _ = activate(total)
            act2_m[...] = act.astype(BF16)

            def shift_arr(step):
                store3(y3, 2 * step, arr[rows(2 * step, 2), :], 2)

            repeat(8, shift_arr)
            whole[rows(0, 2), :] = hid_e[rows(0, 2), :]
            whole[rows(2, 14), :] = hid_m[...]
            whole[rows(16, 2), :] = hid_e[rows(2, 2), :]

            def second_grad(a):
                put_grad(grad, 1, a, outer(whole[rows(a, 16), :], y3[...]))

            def first_grad(a):
                put_grad(grad, 0, a, outer(whole[rows(a, 16), :], z3[...]))

            repeat(3, second_grad)
            fill3(z3, 0, act_e, 1, 1)
            fill3(z3, 1, act_m, 0, 14)
            fill3(z3, 15, act_e, 2, 1)
            whole[rows(0, 1), :] = border[rows(0, 1), :]
            whole[rows(1, 16), :] = sta[...]
            whole[rows(17, 1), :] = border[rows(1, 1), :]
            repeat(3, first_grad)

    by_role(body)


def kernel_d(got_m, got_e, sta, hid_m, hid_e, slope_m, grad_in, w, act2_e, grad, r3, z3, h8):
    def ends(src, first, second, count):
        return jnp.concatenate([src[rows(first, count), :], src[rows(second, count), :]], axis=0)

    def body(leading):
        fill3(r3, 0, got_e, 0, 2)
        fill3(r3, 2, got_m, 0, 2)
        fill3(r3, 4, got_m, 10, 2)
        fill3(r3, 6, got_e, 2, 2)
        for half in range(2):
            total = conv(r3, 4 * half, 2, w, 1 if leading else 0, leading)
            if leading:
                act = total * slope_m[rows(12 * half, 2), :].astype(F32)
                store3(z3, 2 * half, act, 2)
            else:
                act, _ = activate(total)
            act2_e[rows(2 * half, 2), :] = act.astype(BF16)
        if leading:
            h8[rows(0, 2), :] = hid_e[rows(0, 2), :]
            h8[rows(2, 2), :] = hid_m[rows(0, 2), :]
            h8[rows(4, 2), :] = hid_m[rows(12, 2), :]
            h8[rows(6, 2), :] = hid_e[rows(2, 2), :]
            for a in range(3):
                more = outer(ends(h8, a, 4 + a, 2), ends(r3, 0, 6, 2))
                put_grad(grad, 1, a, get_grad(grad_in, 1, a) + more)
                more = outer(ends(sta, a, 12 + a, 2), z3[...])
                put_grad(grad, 0, a, get_grad(grad_in, 0, a) + more)

    by_role(body)


def kernel_e(
    scale, got_e, got_near, got_far, sta, border, slope_e, grad_c, grad_d, w, act2_h, send, keep, r3, z3, x2, tot
):
    has_up, has_down = edge_flags()
    core = lax.axis_index("space_2")

    def emit(src, from_at, to_at, width):
        for pair in range(8):
            for dst, side in ((keep, core), (send, 1 - core)):
                first = pl.multiple_of(32 * pair + 8 * side, 8)
                second = pl.multiple_of(32 * pair + 16 + 8 * side, 8)
                val = jnp.concatenate(
                    [
                        src[pl.ds(first, 8), from_at : from_at + width],
                        src[pl.ds(second, 8), from_at : from_at + width],
                    ],
                    axis=0,
                )
                dst[pl.ds(16 * pair, 16), to_at : to_at + width] = (val * scale).astype(dst.dtype)

    def body(leading):
        store3(r3, 0, above(got_near[...], got_far[...]), 2)
        fill3(r3, 2, got_e, 0, 2)
        fill3(r3, 4, got_e, 2, 2)
        store3(r3, 6, below(got_near[...], got_far[...]), 2)
        spot = lax.broadcasted_iota(jnp.int32, (2 * COLS, CH), 0) // COLS
        for half in range(2):
            total = conv(r3, 4 * half, 2, w, 1 if leading else 0, leading)
            if leading:
                act = total * slope_e[rows(2 * half, 2), :].astype(F32)
            else:
                act, _ = activate(total)
            if half == 0:
                act = act * jnp.where(spot == 0, has_up, 1.0)
            else:
                act = act * jnp.where(spot == 1, has_down, 1.0)
            act2_h[rows(2 * half, 2), :] = act.astype(BF16)
        if leading:
            store3(z3, 0, act2_h[rows(1, 2), :], 2)
            x2[rows(0, 1), :] = border[rows(0, 1), :]
            x2[rows(1, 2), :] = sta[rows(0, 2), :]
            x2[rows(3, 2), :] = sta[rows(14, 2), :]
            x2[rows(5, 1), :] = border[rows(1, 1), :]
            for a in range(3):
                left = jnp.concatenate([x2[rows(a, 1), :], x2[rows(3 + a, 1), :]], axis=0)
                put_grad(tot, 0, a, get_grad(grad_d, 0, a) + outer(left, z3[...]))
            emit(tot, 0, 0, TAPS)
            emit(grad_d, TAPS, TAPS, TAPS)
        else:
            emit(grad_c, 0, 0, 2 * TAPS)

    by_role(body)


def kernel_pick(got_e, inner, outer):
    core = lax.axis_index("space_2")
    inner[...] = got_e[rows(2 * (1 - core), 2), :]
    outer[...] = got_e[rows(2 * core, 2), :]


def kernel_sum(keep, other, total):
    for row in range(0, keep.shape[0], 16):
        part = pl.ds(row, 16)
        total[part, :] = (keep[part, :] + other[part, :].astype(F32)).astype(BF16)


def kernel_f(got_m, got_e, act2_m, act2_e, act2_h, w, out, c3, kept):
    def body(leading):
        fill3(c3, 0, act2_h, 0, 2)
        fill3(c3, 2, act2_e, 0, 2)
        fill3(c3, 4, act2_m, 0, 10)
        fill3(c3, 14, act2_e, 2, 2)
        fill3(c3, 16, act2_h, 2, 2)
        kept[rows(0, 2), :] = got_e[rows(0, 2), :]
        kept[rows(2, 12), :] = got_m[...]
        kept[rows(14, 2), :] = got_e[rows(2, 2), :]

        def block(step):
            row = 4 * step
            total = conv(c3, row, 4, w, 0 if leading else 1, leading)
            out[rows(row, 4), :] = (total + kept[rows(row, 4), :].astype(F32)).astype(BF16)

        repeat(4, block)

    by_role(body)


def call(body, outs, scratch, args, row_units, limit=18, space=pltpu.VMEM, sems=0):
    block = pl.BlockSpec(memory_space=pltpu.VMEM)
    semaphores = [pltpu.SemaphoreType.DMA((sems,))] if sems else []
    return pl.pallas_call(
        body,
        out_shape=[jax.ShapeDtypeStruct(shape, dtype) for shape, dtype in outs],
        in_specs=[pl.BlockSpec(memory_space=space)] * len(args),
        out_specs=[block] * len(outs),
        scratch_shapes=[pltpu.VMEM(shape, dtype) for shape, dtype in scratch] + semaphores,
        compiler_params=pltpu.CompilerParams(vmem_limit_bytes=limit * MIB),
        cost_estimate=pl.CostEstimate(
            flops=int(row_units * 2 * COLS * TAPS * CH),
            bytes_accessed=4 * MIB,
            transcendentals=0,
        ),
    )(*args)


def tick(arrivals, stashed, weights):
    arr = arrivals.reshape(-1, CH)
    sta = stashed.reshape(-1, CH)
    w = weights[0, 0]
    tile = arr.shape[0] // COLS
    space = lax.axis_size(SPACE)
    scale = 1.0 / math.sqrt(tile * space * COLS)

    def img(count, dtype=BF16):
        return ((count * COLS, CH), dtype)

    def img3(count):
        return ((count * COLS, 3 * CH), BF16)

    grad_shape = ((CH, 2 * TAPS), F32)

    two = 2 * COLS
    edge = ((2, two, CH), BF16)
    out_m, act_m, hid_m, slope_m, near, far, sta_v = call(
        kernel_a,
        [img(12), img(14), img(14), img(14), edge, edge, img(16)],
        [img3(16), img3(16), img3(14), (w.shape, BF16), img(16), img(14, F32)],
        (arr, sta, w),
        28,
        limit=LIMIT_A,
        space=pltpu.HBM,
        sems=8,
    )
    sta = sta_v
    hop = [(i, i + 1) for i in range(1, space - 1, 2)]
    hop = hop + [(j, i) for i, j in hop]
    swap = [(0, 1), (1, 0)]
    got_m = lax.ppermute(out_m, "segment", swap)
    near = lax.ppermute(near, "space_2", swap)
    far = lax.ppermute(far, SPACE, hop)
    out_e, act_e, hid_e, slope_e, border = call(
        kernel_b,
        [img(4), img(4), img(4), img(4), img(2)],
        [img3(8), img3(8), img3(8), img(4, F32)],
        (arr, sta, near, far, act_m, w),
        12,
    )
    got_e = lax.ppermute(out_e, "segment", swap)
    act2_m, grad_c = call(
        kernel_c,
        [img(10), grad_shape],
        [img3(12), img3(16), img3(16), img(18)],
        (got_m, arr, sta, border, act_m, act_e, hid_m, hid_e, slope_m, w),
        38,
    )
    got_e, act2_m = lax.optimization_barrier((got_e, act2_m))
    inner_rows, outer_rows = call(kernel_pick, [img(2), img(2)], [], (got_e,), 0, limit=4)
    got_near = lax.ppermute(inner_rows, "space_2", swap)
    got_far = lax.ppermute(outer_rows, SPACE, hop)
    act2_e, grad_d = call(
        kernel_d,
        [img(4), grad_shape],
        [img3(8), img3(4), img(8)],
        (got_m, got_e, sta, hid_m, hid_e, slope_m, grad_c, w),
        12,
    )
    act2_h, sent, keep = call(
        functools.partial(kernel_e, scale),
        [img(4), ((CH // 2, 2 * TAPS), BF16), ((CH // 2, 2 * TAPS), F32)],
        [img3(8), img3(2), img(6), ((CH, TAPS), F32)],
        (got_e, got_near, got_far, sta, border, slope_e, grad_c, grad_d, w),
        8,
    )
    (departing,) = call(
        kernel_f, [img(16)], [img3(18), img(16)], (got_m, got_e, act2_m, act2_e, act2_h, w), 16
    )

    chips = space // 2
    share = CH // space
    other = lax.ppermute(sent, "space_2", swap)
    (pieces,) = call(kernel_sum, [(keep.shape, BF16)], [], (keep, other), 0, limit=8)
    pieces = pieces.reshape(chips, share, 2 * TAPS)
    pieces = lax.all_to_all(pieces, ("space_0", "space_1"), 0, 0, tiled=True)
    owned = jnp.sum(pieces.astype(F32), axis=0)
    owned, departing = lax.optimization_barrier((owned, departing))
    pairs = [(i, i ^ 3) for i in range(4)]
    partner = lax.ppermute(owned.astype(BF16), ("segment", "mirror"), pairs)
    combined = owned + partner.astype(F32)
    return (
        departing.reshape(arrivals.shape),
        combined.reshape(1, 1, share, 2, 3, 3, CH),
    )


def solution(mesh):
    split = Mesh(
        mesh.devices.reshape(mesh.shape["segment"], 4, 4, 2, mesh.shape["mirror"]),
        ("segment", "space_0", "space_1", "space_2", "mirror"),
    )
    in_specs = (
        P("mirror", "segment", SPACE, None, None),
        P("mirror", "segment", SPACE, None, None),
        P("mirror", "segment", None, None, None, None, None),
    )
    out_specs = (
        P("mirror", "segment", SPACE, None, None),
        P("mirror", "segment", SPACE, None, None, None, None),
    )
    return jax.shard_map(tick, mesh=split, in_specs=in_specs, out_specs=out_specs, check_vma=False)
```

```python
import functools
import math

import jax
import jax.numpy as jnp
from jax import lax
from jax.experimental import pallas as pl
from jax.experimental.pallas import tpu as pltpu
from jax.sharding import Mesh
from jax.sharding import PartitionSpec as P

SPACE = ("space_0", "space_1", "space_2")
BF16 = jnp.bfloat16
F32 = jnp.float32
COLS = 128
CH = 256
TAPS = 9 * CH
MIB = 1 << 20
LIMIT_A = 50


def rows(first, count):
    start = first * COLS
    if not isinstance(start, int):
        start = pl.multiple_of(start, COLS)
    return pl.ds(start, count * COLS)


def repeat(steps, body):
    def step(index, carry):
        body(index)
        return carry

    lax.fori_loop(0, steps, step, 0)


def store3(dst, row, val, count):
    size = count * COLS
    col = lax.broadcasted_iota(jnp.int32, (size, CH), 0) & (COLS - 1)
    val = val.astype(F32)
    left = jnp.where(col == 0, 0.0, pltpu.roll(val, 1, 0))
    right = jnp.where(col == COLS - 1, 0.0, pltpu.roll(val, size - 1, 0))
    where = rows(row, count)
    dst[where, 0:CH] = left.astype(BF16)
    dst[where, CH : 2 * CH] = val.astype(BF16)
    dst[where, 2 * CH :] = right.astype(BF16)


def fill3(dst, row, src, first, count):
    for step in range(0, count, 2):
        size = min(2, count - step)
        store3(dst, row + step, src[rows(first + step, size), :], size)


def conv(src3, first, count, weights, which, transposed):
    firsts = first if isinstance(first, tuple) else (first,)
    total = None
    for a in range(3):
        for b in range(3):
            parts = [src3[rows(at + a, count), b * CH : (b + 1) * CH] for at in firsts]
            window = parts[0] if len(parts) == 1 else jnp.concatenate(parts, axis=0)
            if transposed:
                part = lax.dot_general(
                    window,
                    weights[which, 2 - a, 2 - b],
                    (((1,), (1,)), ((), ())),
                    preferred_element_type=F32,
                )
            else:
                part = jnp.dot(window, weights[which, a, b], preferred_element_type=F32)
            total = part if total is None else total + part
    return total


def outer(left, right):
    return lax.dot_general(left, right, (((0,), (0,)), ((), ())), preferred_element_type=F32)


def put_grad(dst, conv_index, a, val):
    for b in range(3):
        at = conv_index * TAPS + (3 * a + b) * CH
        if not isinstance(at, int):
            at = pl.multiple_of(at, CH)
        dst[:, pl.ds(at, CH)] = val[:, (2 - b) * CH : (3 - b) * CH]


def get_grad(src, conv_index, a):
    parts = []
    for b in (2, 1, 0):
        at = conv_index * TAPS + (3 * a + b) * CH
        parts.append(src[:, at : at + CH])
    return jnp.concatenate(parts, axis=1)


def activate(pre):
    sig = 0.5 + 0.5 * jnp.tanh(0.5 * pre)
    return pre * sig, sig * (1.0 + pre * (1.0 - sig))


def is_leading():
    return lax.axis_index("segment") == lax.axis_index("mirror")


def by_role(body):
    leading = is_leading()

    @pl.when(leading)
    def _():
        body(True)

    @pl.when(jnp.logical_not(leading))
    def _():
        body(False)


def edge_flags():
    place = lax.axis_index(SPACE)
    count = lax.axis_size(SPACE)
    return (place > 0).astype(F32), (place < count - 1).astype(F32)


def above(near, far):
    return jnp.where(lax.axis_index("space_2") == 1, near.astype(F32), far.astype(F32))


def below(near, far):
    return jnp.where(lax.axis_index("space_2") == 0, near.astype(F32), far.astype(F32))


def kernel_a(
    arr_hbm, sta_hbm, w_hbm, out_m, act_m, hid_m, slope_m, near, far, sta, s3, a3, c3, w, arr, steep, sems
):
    two = 2 * COLS
    size = arr_hbm.shape[0]
    core = lax.axis_index("space_2")
    inner_at = pl.ds(pl.multiple_of((1 - core) * (size - two), two), two)
    outer_at = pl.ds(pl.multiple_of(core * (size - two), two), two)
    moves = (
        (sta_hbm, sta),
        (w_hbm.at[0], w.at[0]),
        (arr_hbm, arr),
        (w_hbm.at[1], w.at[1]),
        (arr_hbm.at[inner_at], near.at[0]),
        (sta_hbm.at[inner_at], near.at[1]),
        (arr_hbm.at[outer_at], far.at[0]),
        (sta_hbm.at[outer_at], far.at[1]),
    )
    copies = [pltpu.make_async_copy(src, dst, sems.at[i]) for i, (src, dst) in enumerate(moves)]
    for copy in copies:
        copy.start()
    for copy in copies[:2]:
        copy.wait()
    fill3(s3, 0, sta, 2, 12)
    for row in (0, 5):
        hid, slope = activate(conv(s3, row, 5, w, 0, False))
        hid_m[rows(row, 5), :] = hid.astype(BF16)
        slope_m[rows(row, 5), :] = slope.astype(BF16)
        steep[rows(row, 5), :] = slope
    for copy in copies[2:]:
        copy.wait()

    def body(leading):
        fill3(a3, 0, arr, 2, 12)
        for row in (0, 5):
            if leading:
                act, _ = activate(conv(a3, row, 5, w, 0, False))
            else:
                act = conv(a3, row, 5, w, 1, True) * steep[rows(row, 5), :]
            act_m[rows(row, 5), :] = act.astype(BF16)
            store3(c3, row, act, 5)
        for row in (0, 4):
            total = conv(c3, row, 4, w, 1 if leading else 0, not leading)
            out_m[rows(row, 4), :] = (total + arr[rows(4 + row, 4), :].astype(F32)).astype(BF16)

    by_role(body)


def kernel_q(arr, sta, act_m, w, out_q, act_q, hid_q, slope_q, s3, a3, c3, steep):
    fill3(s3, 0, sta, 0, 4)
    fill3(s3, 4, sta, 12, 4)
    hid, slope = activate(conv(s3, (0, 4), 2, w, 0, False))
    hid_q[...] = hid.astype(BF16)
    slope_q[...] = slope.astype(BF16)
    steep[...] = slope

    def body(leading):
        fill3(a3, 0, arr, 0, 4)
        fill3(a3, 4, arr, 12, 4)
        fill3(c3, 2, act_m, 0, 2)
        fill3(c3, 4, act_m, 8, 2)
        if leading:
            act, _ = activate(conv(a3, (0, 4), 2, w, 0, False))
        else:
            act = conv(a3, (0, 4), 2, w, 1, True) * steep[...]
        act_q[...] = act.astype(BF16)
        store3(c3, 0, act[: 2 * COLS], 2)
        store3(c3, 6, act[2 * COLS :], 2)
        total = conv(c3, (0, 4), 2, w, 1 if leading else 0, not leading)
        for half in range(2):
            kept = arr[rows(2 + 10 * half, 2), :].astype(F32)
            out_q[rows(2 * half, 2), :] = (total[2 * half * COLS : (2 * half + 2) * COLS] + kept).astype(BF16)

    by_role(body)


def kernel_b(
    arr, sta, near, far, out_q, act_q, hid_q, slope_q, w, out_e, act_e, hid_e, slope_e, border, s3, a3, c3, steep
):
    has_up, has_down = edge_flags()

    def spread(dst, mid, val):
        val = val.astype(BF16)
        dst[rows(0, 2), :] = val[: 2 * COLS]
        dst[rows(2, 4), :] = mid[...]
        dst[rows(6, 2), :] = val[2 * COLS :]

    up, down = above(near[1], far[1]), below(near[1], far[1])
    border[rows(0, 1), :] = up[COLS:].astype(BF16)
    border[rows(1, 1), :] = down[:COLS].astype(BF16)
    store3(s3, 0, up, 2)
    fill3(s3, 2, sta, 0, 2)
    fill3(s3, 4, sta, 14, 2)
    store3(s3, 6, down, 2)
    spot = lax.broadcasted_iota(jnp.int32, (4 * COLS, CH), 0) // COLS
    mask = jnp.where(spot == 0, has_up, jnp.where(spot == 3, has_down, 1.0))
    hid, slope = activate(conv(s3, (0, 4), 2, w, 0, False))
    spread(hid_e, hid_q, hid * mask)
    spread(slope_e, slope_q, slope)
    steep[...] = slope * mask

    def body(leading):
        store3(a3, 0, above(near[0], far[0]), 2)
        fill3(a3, 2, arr, 0, 2)
        fill3(a3, 4, arr, 14, 2)
        store3(a3, 6, below(near[0], far[0]), 2)
        fill3(c3, 2, act_q, 0, 2)
        fill3(c3, 4, act_q, 2, 2)
        if leading:
            act, _ = activate(conv(a3, (0, 4), 2, w, 0, False))
            spot = lax.broadcasted_iota(jnp.int32, (4 * COLS, CH), 0) // COLS
            act = act * jnp.where(spot == 0, has_up, jnp.where(spot == 3, has_down, 1.0))
        else:
            act = conv(a3, (0, 4), 2, w, 1, True) * steep[...]
        spread(act_e, act_q, act)
        store3(c3, 0, act[: 2 * COLS], 2)
        store3(c3, 6, act[2 * COLS :], 2)
        total = conv(c3, (0, 4), 2, w, 1 if leading else 0, not leading)
        for half in range(2):
            kept = arr[rows(14 * half, 2), :].astype(F32)
            part = total[2 * half * COLS : (2 * half + 2) * COLS] + kept
            out_e[rows(6 * half, 2), :] = part.astype(BF16)
        out_e[rows(2, 4), :] = out_q[...]

    by_role(body)


def kernel_c(
    got_m, arr, sta, border, act_m, act_e, hid_m, hid_e, slope_m, w, act2_m, grad, r3, y3, z3, whole
):
    def body(leading):
        fill3(r3, 0, got_m, 0, 8)
        total = conv(r3, 0, 6, w, 1 if leading else 0, leading)
        if leading:
            act = total * slope_m[rows(2, 6), :].astype(F32)
            act2_m[...] = act.astype(BF16)
            store3(z3, 0, act, 6)
            for a in range(3):
                put_grad(grad, 1, a, outer(hid_m[rows(a, 8), :], r3[rows(0, 8), :]))
                put_grad(grad, 0, a, outer(sta[rows(4 + a, 6), :], z3[rows(0, 6), :]))
        else:
            act, _ = activate(total)
            act2_m[...] = act.astype(BF16)

            def shift_arr(step):
                store3(y3, 2 * step, arr[rows(2 * step, 2), :], 2)

            repeat(8, shift_arr)
            whole[rows(0, 4), :] = hid_e[rows(0, 4), :]
            whole[rows(4, 10), :] = hid_m[...]
            whole[rows(14, 4), :] = hid_e[rows(4, 4), :]

            def second_grad(a):
                put_grad(grad, 1, a, outer(whole[rows(a, 16), :], y3[...]))

            def first_grad(a):
                put_grad(grad, 0, a, outer(whole[rows(a, 16), :], z3[...]))

            repeat(3, second_grad)
            fill3(z3, 0, act_e, 1, 3)
            fill3(z3, 3, act_m, 0, 10)
            fill3(z3, 13, act_e, 4, 3)
            whole[rows(0, 1), :] = border[rows(0, 1), :]
            whole[rows(1, 16), :] = sta[...]
            whole[rows(17, 1), :] = border[rows(1, 1), :]
            repeat(3, first_grad)

    by_role(body)


def kernel_d(got_m, got_e, sta, hid_m, hid_e, slope_m, slope_e, grad_in, w, act2_e, grad, r3, z3, h6):
    def body(leading):
        fill3(r3, 0, got_e, 0, 4)
        fill3(r3, 4, got_m, 0, 2)
        fill3(r3, 6, got_m, 6, 2)
        fill3(r3, 8, got_e, 4, 4)
        for half in range(2):
            total = conv(r3, 6 * half, 4, w, 1 if leading else 0, leading)
            if leading:
                if half == 0:
                    slope = jnp.concatenate([slope_e[rows(2, 2), :], slope_m[rows(0, 2), :]], axis=0)
                else:
                    slope = jnp.concatenate([slope_m[rows(8, 2), :], slope_e[rows(4, 2), :]], axis=0)
                act = total * slope.astype(F32)
                store3(z3, 4 * half, act, 4)
            else:
                act, _ = activate(total)
            act2_e[rows(4 * half, 4), :] = act.astype(BF16)
        if leading:
            h6[rows(0, 4), :] = hid_e[rows(0, 4), :]
            h6[rows(4, 2), :] = hid_m[rows(0, 2), :]
            h6[rows(6, 2), :] = hid_m[rows(8, 2), :]
            h6[rows(8, 4), :] = hid_e[rows(4, 4), :]
            for a in range(3):
                more = outer(h6[rows(a, 4), :], r3[rows(0, 4), :])
                more = more + outer(h6[rows(6 + a, 4), :], r3[rows(8, 4), :])
                put_grad(grad, 1, a, get_grad(grad_in, 1, a) + more)
                more = outer(sta[rows(a, 4), :], z3[rows(0, 4), :])
                more = more + outer(sta[rows(10 + a, 4), :], z3[rows(4, 4), :])
                put_grad(grad, 0, a, get_grad(grad_in, 0, a) + more)

    by_role(body)


def kernel_e(
    scale, got_e, got_near, got_far, sta, border, slope_e, grad_c, grad_d, w, act2_h, send, keep, r3, z3, x2, tot
):
    has_up, has_down = edge_flags()
    core = lax.axis_index("space_2")

    def emit(src, from_at, to_at, width):
        for pair in range(8):
            for dst, side in ((keep, core), (send, 1 - core)):
                first = pl.multiple_of(32 * pair + 8 * side, 8)
                second = pl.multiple_of(32 * pair + 16 + 8 * side, 8)
                val = jnp.concatenate(
                    [
                        src[pl.ds(first, 8), from_at : from_at + width],
                        src[pl.ds(second, 8), from_at : from_at + width],
                    ],
                    axis=0,
                )
                dst[pl.ds(16 * pair, 16), to_at : to_at + width] = (val * scale).astype(dst.dtype)

    def body(leading):
        store3(r3, 0, above(got_near[...], got_far[...]), 2)
        fill3(r3, 2, got_e, 0, 2)
        fill3(r3, 4, got_e, 6, 2)
        store3(r3, 6, below(got_near[...], got_far[...]), 2)
        spot = lax.broadcasted_iota(jnp.int32, (2 * COLS, CH), 0) // COLS
        for half in range(2):
            total = conv(r3, 4 * half, 2, w, 1 if leading else 0, leading)
            if leading:
                act = total * slope_e[rows(6 * half, 2), :].astype(F32)
            else:
                act, _ = activate(total)
            if half == 0:
                act = act * jnp.where(spot == 0, has_up, 1.0)
            else:
                act = act * jnp.where(spot == 1, has_down, 1.0)
            act2_h[rows(2 * half, 2), :] = act.astype(BF16)
        if leading:
            store3(z3, 0, act2_h[rows(1, 2), :], 2)
            x2[rows(0, 1), :] = border[rows(0, 1), :]
            x2[rows(1, 2), :] = sta[rows(0, 2), :]
            x2[rows(3, 2), :] = sta[rows(14, 2), :]
            x2[rows(5, 1), :] = border[rows(1, 1), :]
            for a in range(3):
                left = jnp.concatenate([x2[rows(a, 1), :], x2[rows(3 + a, 1), :]], axis=0)
                put_grad(tot, 0, a, get_grad(grad_d, 0, a) + outer(left, z3[...]))
            emit(tot, 0, 0, TAPS)
            emit(grad_d, TAPS, TAPS, TAPS)
        else:
            emit(grad_c, 0, 0, 2 * TAPS)

    by_role(body)


def kernel_pick(got_e, inner, outer):
    core = lax.axis_index("space_2")
    inner[...] = got_e[rows(6 * (1 - core), 2), :]
    outer[...] = got_e[rows(6 * core, 2), :]


def kernel_sum(keep, other, total):
    for row in range(0, keep.shape[0], 16):
        part = pl.ds(row, 16)
        total[part, :] = (keep[part, :] + other[part, :].astype(F32)).astype(BF16)


def kernel_f(got_m, got_e, act2_m, act2_e, act2_h, w, out, c3, kept):
    def body(leading):
        fill3(c3, 0, act2_h, 0, 2)
        fill3(c3, 2, act2_e, 0, 4)
        fill3(c3, 6, act2_m, 0, 6)
        fill3(c3, 12, act2_e, 4, 4)
        fill3(c3, 16, act2_h, 2, 2)
        kept[rows(0, 4), :] = got_e[rows(0, 4), :]
        kept[rows(4, 8), :] = got_m[...]
        kept[rows(12, 4), :] = got_e[rows(4, 4), :]

        def block(step):
            row = 4 * step
            total = conv(c3, row, 4, w, 0 if leading else 1, leading)
            out[rows(row, 4), :] = (total + kept[rows(row, 4), :].astype(F32)).astype(BF16)

        repeat(4, block)

    by_role(body)


def call(body, outs, scratch, args, row_units, limit=18, space=pltpu.VMEM, sems=0):
    block = pl.BlockSpec(memory_space=pltpu.VMEM)
    semaphores = [pltpu.SemaphoreType.DMA((sems,))] if sems else []
    return pl.pallas_call(
        body,
        out_shape=[jax.ShapeDtypeStruct(shape, dtype) for shape, dtype in outs],
        in_specs=[pl.BlockSpec(memory_space=space)] * len(args),
        out_specs=[block] * len(outs),
        scratch_shapes=[pltpu.VMEM(shape, dtype) for shape, dtype in scratch] + semaphores,
        compiler_params=pltpu.CompilerParams(vmem_limit_bytes=limit * MIB),
        cost_estimate=pl.CostEstimate(
            flops=int(row_units * 2 * COLS * TAPS * CH),
            bytes_accessed=4 * MIB,
            transcendentals=0,
        ),
    )(*args)


def tick(arrivals, stashed, weights):
    arr = arrivals.reshape(-1, CH)
    sta = stashed.reshape(-1, CH)
    w = weights[0, 0]
    tile = arr.shape[0] // COLS
    space = lax.axis_size(SPACE)
    scale = 1.0 / math.sqrt(tile * space * COLS)

    def img(count, dtype=BF16):
        return ((count * COLS, CH), dtype)

    def img3(count):
        return ((count * COLS, 3 * CH), BF16)

    grad_shape = ((CH, 2 * TAPS), F32)

    two = 2 * COLS
    edge = ((2, two, CH), BF16)
    out_m, act_m, hid_m, slope_m, near, far, sta_v = call(
        kernel_a,
        [img(8), img(10), img(10), img(10), edge, edge, img(16)],
        [img3(12), img3(12), img3(10), (w.shape, BF16), img(16), img(10, F32)],
        (arr, sta, w),
        28,
        limit=LIMIT_A,
        space=pltpu.HBM,
        sems=8,
    )
    sta = sta_v
    hop = [(i, i + 1) for i in range(1, space - 1, 2)]
    hop = hop + [(j, i) for i, j in hop]
    swap = [(0, 1), (1, 0)]
    got_m = lax.ppermute(out_m, "segment", swap)
    near = lax.ppermute(near, "space_2", swap)
    far = lax.ppermute(far, SPACE, hop)
    quad = call(
        kernel_q,
        [img(4), img(4), img(4), img(4)],
        [img3(8), img3(8), img3(8), img(4, F32)],
        (arr, sta, act_m, w),
        12,
    )
    out_e, act_e, hid_e, slope_e, border = call(
        kernel_b,
        [img(8), img(8), img(8), img(8), img(2)],
        [img3(8), img3(8), img3(8), img(4, F32)],
        (arr, sta, near, far, *quad, w),
        12,
    )
    got_e = lax.ppermute(out_e, "segment", swap)
    inner_rows, outer_rows = call(kernel_pick, [img(2), img(2)], [], (got_e,), 0, limit=4)
    got_near = lax.ppermute(inner_rows, "space_2", swap)
    got_far = lax.ppermute(outer_rows, SPACE, hop)
    act2_m, grad_c = call(
        kernel_c,
        [img(6), grad_shape],
        [img3(8), img3(16), img3(16), img(18)],
        (got_m, arr, sta, border, act_m, act_e, hid_m, hid_e, slope_m, w),
        38,
    )
    act2_e, grad_d = call(
        kernel_d,
        [img(8), grad_shape],
        [img3(12), img3(8), img(12)],
        (got_m, got_e, sta, hid_m, hid_e, slope_m, slope_e, grad_c, w),
        24,
    )
    act2_h, sent, keep = call(
        functools.partial(kernel_e, scale),
        [img(4), ((CH // 2, 2 * TAPS), BF16), ((CH // 2, 2 * TAPS), F32)],
        [img3(8), img3(2), img(6), ((CH, TAPS), F32)],
        (got_e, got_near, got_far, sta, border, slope_e, grad_c, grad_d, w),
        8,
    )
    (departing,) = call(
        kernel_f, [img(16)], [img3(18), img(16)], (got_m, got_e, act2_m, act2_e, act2_h, w), 16
    )

    chips = space // 2
    share = CH // space
    other = lax.ppermute(sent, "space_2", swap)
    (pieces,) = call(kernel_sum, [(keep.shape, BF16)], [], (keep, other), 0, limit=8)
    pieces = pieces.reshape(chips, share, 2 * TAPS)
    pieces = lax.all_to_all(pieces, ("space_0", "space_1"), 0, 0, tiled=True)
    owned = jnp.sum(pieces.astype(F32), axis=0)
    owned, departing = lax.optimization_barrier((owned, departing))
    pairs = [(i, i ^ 3) for i in range(4)]
    partner = lax.ppermute(owned.astype(BF16), ("segment", "mirror"), pairs)
    combined = owned + partner.astype(F32)
    return (
        departing.reshape(arrivals.shape),
        combined.reshape(1, 1, share, 2, 3, 3, CH),
    )


def solution(mesh):
    split = Mesh(
        mesh.devices.reshape(mesh.shape["segment"], 4, 4, 2, mesh.shape["mirror"]),
        ("segment", "space_0", "space_1", "space_2", "mirror"),
    )
    in_specs = (
        P("mirror", "segment", SPACE, None, None),
        P("mirror", "segment", SPACE, None, None),
        P("mirror", "segment", None, None, None, None, None),
    )
    out_specs = (
        P("mirror", "segment", SPACE, None, None),
        P("mirror", "segment", SPACE, None, None, None, None),
    )
    return jax.shard_map(tick, mesh=split, in_specs=in_specs, out_specs=out_specs, check_vma=False)
```
